32 devices in a mesh: section: 2 (over core), expert: 4 (over z), tensor: 4 (over y, x).
Axes of the slice: x: 2, y: 2, z: 4, core: 2. Of those that a mesh axis runs over, the one named last changes fastest.
Arguments:
- x_in: bfloat16 [2, 4096, 768], P(None, 'expert'), may hold values from -6 to 6
- cotangent: bfloat16 [2, 4096, 768], P(None, 'expert'), may hold values from -6 to 6
- attn_gain: bfloat16 [2, 768], P('section'), may hold values from 0.5 to 1.5
- ffn_gain: bfloat16 [2, 768], P('section'), may hold values from 0.5 to 1.5
- w_query: bfloat16 [2, 768, 768], P('section', None, 'tensor'), may hold values from -0.21875 to 0.21875
- w_key: bfloat16 [2, 768, 768], P('section', None, 'tensor'), may hold values from -0.21875 to 0.21875
- w_value: bfloat16 [2, 768, 768], P('section', None, 'tensor'), may hold values from -0.21875 to 0.21875
- w_out: bfloat16 [2, 768, 768], P('section', 'tensor'), may hold values from -2.140625 to 2.140625
- rel_bias: bfloat16 [2, 32, 12], P('section', None, 'tensor'), may hold values from -5 to 5
- w_router: bfloat16 [2, 768, 16], P('section'), may hold values from -0.21875 to 0.21875
- w_in: bfloat16 [2, 16, 768, 3072], P('section', 'expert', None, 'tensor'), may hold values from -0.21875 to 0.21875
- w_back: bfloat16 [2, 16, 3072, 768], P('section', 'expert', 'tensor'), may hold values from -2.46875 to 2.46875
- routes: int32 [2, 2, 4096, 1], P('section', None, 'expert'), may hold values from 0 to 15; in each aligned block of 1024 rows (0 to 1023, 1024 to 2047, ..., all dimensions but the last counted through in order) at most 96 rows name the same one
- keep_mask: int32 [2, 2, 4096], P('section', None, 'expert'), may hold values 0 or 1
Outputs:
- acts: bfloat16 [2, 2, 4096, 768], P('section', None, 'expert')
- input_grads: bfloat16 [2, 2, 4096, 768], P('section', None, 'expert')
- g_attn_gain: float32 [2, 768], P('section', 'expert')
- g_ffn_gain: float32 [2, 768], P('section', 'expert')
- g_query: float32 [2, 768, 768], P('section', 'expert', 'tensor')
- g_key: float32 [2, 768, 768], P('section', 'expert', 'tensor')
- g_value: float32 [2, 768, 768], P('section', 'expert', 'tensor')
- g_out: float32 [2, 768, 768], P('section', 'tensor', 'expert')
- g_rel: float32 [2, 32, 12], P('section', 'expert', 'tensor')
- g_router: float32 [2, 768, 16], P('section', 'expert')
- g_in: float32 [2, 16, 768, 3072], P('section', 'expert', None, 'tensor')
- g_back: float32 [2, 16, 3072, 768], P('section', 'expert', 'tensor')
The draws below stay inside these ranges and needn't reach their ends.
Inputs may be any that keep to these rules, and one draw needn't show every extreme that they name: `routes`: in each aligned block of 1024 tokens (one index of the expert axis, one section and micro-batch), no expert is named more than 96 times, and some block reaches 96.
All inputs are finite; a program needn't handle non-finite values. No bound on the sum of `keep_mask` on one device may be relied on, other than what follows from the above.
Results may differ from the reference program's by a relative error of at most 0.04.
Values may be sent and summed in bfloat16 or wider, within the bound.
No kernel may reach another device: no remote copies, remote signals or barrier semaphores. Data moves between devices by JAX's collectives and lax.ppermute only.
A program may use at most 384 MiB of HBM per device.

```python
import math
import jax
import jax.numpy as jnp
import numpy as np
from jax import lax

D = 768
H = 12
DH = 64
FF = 3072
NB = 32
LENGTH = 512
MB = 2
TOK_DEV = 1024
EXPERTS = 16
TOKENS = 4096
CAP = 96
N_EXPERT = 4


def place_ends(entries, own_key, smallest, top_value):
    extent = entries.shape
    place = [jax.random.randint(jax.random.fold_in(own_key, axis), (), 0, extent[axis]) for axis in range(len(extent))]
    entries = entries.at[tuple(place)].set(smallest)
    longest = extent.index(max(extent))
    place[longest] = (place[longest] + 1) % extent[longest]
    return entries.at[tuple(place)].set(top_value)


def block_scale(stream_key, extent, split, smallest, largest):
    level, own = 1.0, jax.random.fold_in(stream_key, 6)
    for axis_at, parts in split:
        heights = jnp.exp(jax.random.uniform(jax.random.fold_in(own, axis_at), (parts,), jnp.float32, smallest / len(split), largest / len(split)))
        level = level * jnp.repeat(heights, extent[axis_at] // parts).reshape([-1 if axis == axis_at else 1 for axis in range(len(extent))])
    return level


def assign_block(key, own, number, rows, count, top, bound, skew):
    sequence = jax.random.permutation(key, count)
    crowded, usual = shares(count, rows * top, bound, skew, True), shares(count, rows * top, bound, skew, False)
    places = jnp.arange(count)

    def named(tallies, offset_by):
        used = int((tallies > 0).sum())
        fixed = max(1, used // 4)
        moved = fixed + (places - fixed + offset_by * (used - fixed)) % max(1, count - fixed)
        return jnp.zeros((count,), jnp.int32).at[sequence[jnp.where(places < fixed, places, moved)]].set(jnp.asarray(tallies, jnp.int32))

    tallies = jnp.where(number % 4 == 0, named(crowded, number // 4), named(usual, number - number // 4 - 1))
    mixed = jax.random.permutation(jax.random.fold_in(own, 3), count)
    donor, receiver = mixed[0:count // 2 * 2:2], mixed[1:count // 2 * 2:2]
    margin = jnp.minimum(tallies[donor] - 1, bound - tallies[receiver]) // 2
    margin = jnp.where((donor == sequence[0]) | (receiver == sequence[0]) | (tallies[receiver] == 0), 0, jnp.maximum(margin, 0))
    moved = jax.random.randint(jax.random.fold_in(own, 4), (count // 2,), 0, 1 << 20) % (margin + 1)
    tallies = tallies.at[donor].add(-moved).at[receiver].add(moved)
    labels = jnp.searchsorted(jnp.cumsum(tallies), jnp.arange(rows * top), side="right").astype(jnp.int32)
    table = labels.reshape(top, rows).T
    table = table[jax.random.permutation(jax.random.fold_in(own, 1), rows)]
    offset_by = jax.random.randint(jax.random.fold_in(own, 2), (rows, 1), 0, top)
    return jnp.take_along_axis(table, (jnp.arange(top)[None, :] + offset_by) % top, axis=1)


def shares(number_of, total, reach, lean, full):
    loads = [(1 << 20) // math.isqrt(standing ** lean) + 1 for standing in range(1, number_of + 1)]
    largest = reach if full else min(reach, max(-(-total // number_of), total * loads[0] // sum(loads)))
    least = 1 if total - largest >= number_of - 1 else 0
    given, spare = [largest] + [least] * (number_of - 1), total - largest - least * (number_of - 1)
    while spare > 0:
        candidates = [i for i in range(1, number_of) if given[i] < largest] or [i for i in range(1, number_of) if given[i] < reach]
        mass, remaining = sum([loads[i] for i in candidates]), spare
        for i in candidates:
            addition = min(reach - given[i], max(1, remaining * loads[i] // mass), spare)
            given[i] = given[i] + addition
            spare = spare - addition
    return np.array(given)


def normal_values(key, dims, width, most, shards=(), kind=jnp.bfloat16):
    result = jax.random.normal(key, dims, jnp.float32) * width
    if len(shards) > 0:
        result = block_scale(key, dims, shards, -0.22, 0.18) * result
    return jnp.clip(result, min=-most, max=most).astype(kind)


def setup_inputs(seed: int = 0) -> dict:
    key_of = jax.random.split(jax.random.key(seed), 15)
    x_in = normal_values(key_of[0], (MB, TOKENS, D), 1.0, 6.0, ((1, 4),))
    cotangent = normal_values(key_of[1], (MB, TOKENS, D), 1.0, 6.0, ((1, 4),))
    attn_gain = jnp.clip(1.0 + 0.1 * jax.random.normal(key_of[2], (2, D), jnp.float32), 0.5, 1.5).astype(jnp.bfloat16)
    ffn_gain = jnp.clip(1.0 + 0.1 * jax.random.normal(key_of[3], (2, D), jnp.float32), 0.5, 1.5).astype(jnp.bfloat16)
    w_query = normal_values(key_of[4], (2, D, H * DH), D ** -0.5, 0.21875, ((0, 2), (2, 4)))
    w_key = normal_values(key_of[5], (2, D, H * DH), D ** -0.5, 0.21875, ((0, 2), (2, 4)))
    w_value = normal_values(key_of[6], (2, D, H * DH), D ** -0.5, 0.21875, ((0, 2), (2, 4)))
    w_out = normal_values(key_of[7], (2, H * DH, D), ((LENGTH / 4000) ** 0.5), 2.140625, ((0, 2), (1, 4)))
    rel_bias = normal_values(key_of[8], (2, NB, H), 1.0, 5.0, ((0, 2), (2, 4)))
    w_router = normal_values(key_of[9], (2, D, EXPERTS), D ** -0.5, 0.21875, ((0, 2),))
    w_in = normal_values(key_of[10], (2, EXPERTS, D, FF), D ** -0.5, 0.21875, ((0, 2), (1, 4), (3, 4)))
    w_back = normal_values(key_of[11], (2, EXPERTS, FF, D), (EXPERTS / (0.7 * FF ** 0.5)), 2.46875, ((0, 2), (1, 4), (2, 4)))
    routes_keys = jax.random.split(jax.random.fold_in(key_of[12], 1), 2 * MB * TOKENS // TOK_DEV)
    routes_turns = jax.random.permutation(jax.random.fold_in(key_of[12], 3), 2 * MB * TOKENS // TOK_DEV)
    routes = jax.vmap(lambda own, number: assign_block(jax.random.fold_in(key_of[12], 2), own, number, TOK_DEV, EXPERTS, 1, CAP, 2))(routes_keys, routes_turns).reshape((2, MB, TOKENS, 1))
    keep_mask = place_ends((jax.random.randint(key_of[13], (2, MB, TOKENS), 0, 8) < 7).astype(jnp.int32), jax.random.fold_in(key_of[13], 1), 0, 1)
    return {"x_in": x_in, "cotangent": cotangent, "attn_gain": attn_gain, "ffn_gain": ffn_gain, "w_query": w_query, "w_key": w_key, "w_value": w_value, "w_out": w_out, "rel_bias": rel_bias, "w_router": w_router, "w_in": w_in, "w_back": w_back, "routes": routes, "keep_mask": keep_mask}


EPSILON = 1e-06
HIGHEST = lax.Precision.HIGHEST

@jax.custom_vjp
def low(v):
    return lax.optimization_barrier(v.astype(jnp.bfloat16)).astype(jnp.float32)

@jax.custom_vjp
def low_back(v):
    return v

def low_keep(v):
    return (low(v), None)

def low_pass(kept, grad):
    return (grad,)

def back_keep(v):
    return (v, None)

def back_low(kept, grad):
    return (low(grad),)
low.defvjp(low_keep, low_pass)
low_back.defvjp(back_keep, back_low)

def relative_buckets(seq_length):
    bucket_list = []
    for offset in range(-(seq_length - 1), seq_length):
        bucket = 16 if offset > 0 else 0
        distance = abs(offset)
        if distance < 8:
            bucket = bucket + distance
        else:
            ladder = 0
            while ladder < 7 and distance ** 8 >= 2 ** (24 + 4 * (ladder + 1)):
                ladder = ladder + 1
            bucket = bucket + 8 + ladder
        bucket_list.append(bucket)
    return np.array(bucket_list, dtype=np.int32)

def matmul(left, right):
    return jnp.dot(left, right, precision=HIGHEST)

def normalize(values, gain):
    return values * lax.rsqrt(lax.optimization_barrier(jnp.mean(values * values, axis=-1, keepdims=True)) + EPSILON) * gain

def attention(query, key, value, offsets):
    sequences = TOKENS // LENGTH
    grid = (np.arange(LENGTH)[None, :] - np.arange(LENGTH)[:, None] + (LENGTH - 1)).astype(np.int32)
    bias = jnp.transpose(offsets[grid], (2, 0, 1))

    def one_sequence(inputs):
        queries, keys, values = inputs
        scores = low_back(0.125 * jnp.einsum('qhd,khd->hqk', queries, keys, precision=HIGHEST) + bias)
        probs = jax.nn.softmax(scores, axis=-1)
        return jnp.einsum('hqk,khd->qhd', low(probs), values, precision=HIGHEST)
    shaped = (query.reshape(sequences, LENGTH, H, DH), key.reshape(sequences, LENGTH, H, DH), value.reshape(sequences, LENGTH, H, DH))
    mixed = lax.map(jax.checkpoint(one_sequence), shaped)
    return mixed.reshape(TOKENS, H * DH)

def layer(inputs, params, route_rows, keep_rows, table):
    attn_gain, ffn_gain, w_query, w_key, w_value, w_out, rel, w_router, w_in, w_back = params
    normed = low(normalize(inputs, attn_gain))
    query = low_back(low(matmul(normed, w_query)))
    key = low_back(low(matmul(normed, w_key)))
    value = low_back(low(matmul(normed, w_value)))
    mixed = low_back(low(attention(query, key, value, rel[table])))
    middle = inputs + low_back(matmul(mixed, w_out))
    normed_two = low(normalize(middle, ffn_gain))
    logits = low_back(matmul(normed_two, w_router))
    probs = jax.nn.softmax(logits, axis=-1)
    chosen = route_rows[:, None] == jnp.arange(EXPERTS, dtype=jnp.int32)[None, :]
    gate = lax.optimization_barrier(jnp.sum(probs * chosen.astype(jnp.float32), axis=-1))
    kept = keep_rows.astype(jnp.float32)
    counts = chosen.astype(jnp.int32).reshape(N_EXPERT, TOK_DEV, EXPERTS)
    running = jnp.cumsum(counts, axis=1, dtype=jnp.int32).astype(jnp.int32)
    rank = lax.optimization_barrier(jnp.sum((running - 1) * counts, axis=-1, dtype=jnp.int32)).astype(jnp.int32).reshape(TOKENS)
    source = jnp.arange(TOKENS, dtype=jnp.int32) // TOK_DEV
    slot = (route_rows.astype(jnp.int32) * (N_EXPERT * CAP) + source * CAP + rank).astype(jnp.int32)
    dispatched = jnp.zeros((EXPERTS * N_EXPERT * CAP, D), jnp.float32).at[slot].add(low_back(normed_two) * kept[:, None])
    inner = jnp.einsum('esd,edf->esf', dispatched.reshape(EXPERTS, N_EXPERT * CAP, D), w_in, precision=HIGHEST)
    hidden = low(jax.nn.gelu(low_back(inner), approximate=False))
    expert_out = low_back(low(jnp.einsum('esf,efd->esd', hidden, w_back, precision=HIGHEST)))
    per_token = expert_out.reshape(EXPERTS * N_EXPERT * CAP, D)[slot]
    return middle + (kept * gate)[:, None] * per_token

def reference(x_in, cotangent, attn_gain, ffn_gain, w_query, w_key, w_value, w_out, rel_bias, w_router, w_in, w_back, routes, keep_mask):
    table = relative_buckets(LENGTH)
    arrays = (attn_gain, ffn_gain, w_query, w_key, w_value, w_out, rel_bias, w_router, w_in, w_back)
    params = tuple((tuple((item[section].astype(jnp.float32) for item in arrays)) for section in range(2)))
    acts_list = []
    grads_list = []
    totals = None
    for batch in range(MB):

        def forward(rows, extra, weights):
            first = layer(rows, weights[0], routes[0, batch, :, 0], keep_mask[0, batch], table)
            shown = low(first)
            second = layer(low_back(shown + extra), weights[1], routes[1, batch, :, 0], keep_mask[1, batch], table)
            return (second, shown)
        second, pull, shown = jax.vjp(forward, x_in[batch].astype(jnp.float32), jnp.zeros((TOKENS, D), jnp.float32), params, has_aux=True)
        input_grad, middle_grad, param_grads = pull(cotangent[batch].astype(jnp.float32))
        acts_list.append(jnp.stack([shown, second]).astype(jnp.bfloat16))
        grads_list.append(jnp.stack([input_grad, middle_grad]).astype(jnp.bfloat16))
        totals = param_grads if totals is None else jax.tree.map(jnp.add, totals, param_grads)
    acts = jnp.stack(acts_list, axis=1)
    input_grads = jnp.stack(grads_list, axis=1)
    stacked = [jnp.stack([totals[0][number], totals[1][number]]) for number in range(10)]
    return (acts, input_grads, stacked[0], stacked[1], stacked[2], stacked[3], stacked[4], stacked[5], stacked[6], stacked[7], stacked[8], stacked[9])
```

```python
import functools
import jax
import jax.numpy as jnp
import numpy as np
from jax import lax
from jax.experimental import pallas as pl
from jax.experimental.pallas import tpu as pltpu
from jax.sharding import PartitionSpec as P

DH = 64
LENGTH = 512
TILE = 128
EPSILON = 1e-06
BF16 = jnp.bfloat16
F32 = jnp.float32


def bucket_starts():
    starts = list(range(1, 9))
    for ladder in range(1, 8):
        distance = 8
        while distance**8 < 2 ** (24 + 4 * ladder):
            distance = distance + 1
        starts.append(distance)
    return starts


STARTS = bucket_starts()
HALF = len(STARTS) + 1


def root_mean(values):
    return lax.rsqrt(jnp.mean(values * values, axis=-1, keepdims=True) + EPSILON)


def dot(left, right):
    return jnp.dot(left, right, preferred_element_type=F32)


def dot_left(left, right):
    return lax.dot_general(left, right, (((0,), (0,)), ((), ())), preferred_element_type=F32)


def dot_right(left, right):
    return lax.dot_general(left, right, (((1,), (1,)), ((), ())), preferred_element_type=F32)


def offset_block(delta):
    rows = lax.broadcasted_iota(jnp.int32, (TILE, TILE), 0)
    cols = lax.broadcasted_iota(jnp.int32, (TILE, TILE), 1)
    return rows - cols + delta * TILE


def fill_bias(rel_ref, bias_ref, heads):
    tiles = LENGTH // TILE
    for delta in (-1, 0, 1):
        offset = offset_block(delta)
        blocks = [jnp.full((TILE, TILE), rel_ref[0, h], F32) for h in range(heads)]
        for step, start in enumerate(STARTS):
            if delta <= 0:
                mask = offset <= -start
                blocks = [
                    jnp.where(mask, rel_ref[step + 1, h], block) for h, block in enumerate(blocks)
                ]
            if delta >= 0:
                mask = offset >= start
                blocks = [
                    jnp.where(mask, rel_ref[HALF + step + 1, h], block)
                    for h, block in enumerate(blocks)
                ]
        for h in range(heads):
            for i in range(tiles):
                j = i - delta
                if 0 <= j < tiles:
                    bias_ref[h, i * TILE : (i + 1) * TILE, j * TILE : (j + 1) * TILE] = blocks[h]
    for h in range(heads):
        above = jnp.full((TILE, TILE), rel_ref[2 * HALF - 1, h], F32)
        below = jnp.full((TILE, TILE), rel_ref[HALF - 1, h], F32)
        for i in range(tiles):
            for j in range(tiles):
                if abs(i - j) > 1:
                    bias_ref[h, i * TILE : (i + 1) * TILE, j * TILE : (j + 1) * TILE] = (
                        above if i > j else below
                    )


def attend_kernel(rel_ref, qkv_ref, mixed_ref, lse_ref, bias_ref, *, heads):
    @pl.when(pl.program_id(0) == 0)
    def _():
        fill_bias(rel_ref, bias_ref, heads)

    cols = heads * DH
    outs = []
    for h in range(heads):
        query = qkv_ref[:, h * DH : (h + 1) * DH]
        keys = qkv_ref[:, cols + h * DH : cols + (h + 1) * DH]
        values = qkv_ref[:, 2 * cols + h * DH : 2 * cols + (h + 1) * DH]
        scores = dot_right(keys, query) * 0.125 + bias_ref[h]
        highest = jnp.max(scores, axis=0, keepdims=True)
        raised = jnp.exp(scores - highest)
        total = jnp.sum(raised, axis=0, keepdims=True)
        probs = (raised * (1.0 / total)).astype(BF16)
        outs.append(dot_left(probs, values).astype(BF16))
        lse_ref[0, h : h + 1, :] = highest + jnp.log(total)
    mixed_ref[...] = jnp.concatenate(outs, axis=1)


def attend(qkv, rel):
    rows = qkv.shape[0]
    heads = rel.shape[1]
    cols = heads * DH
    sequences = rows // LENGTH
    return pl.pallas_call(
        functools.partial(attend_kernel, heads=heads),
        grid=(sequences,),
        in_specs=[
            pl.BlockSpec(memory_space=pltpu.SMEM),
            pl.BlockSpec((LENGTH, 3 * cols), lambda s: (s, 0)),
        ],
        out_specs=[
            pl.BlockSpec((LENGTH, cols), lambda s: (s, 0)),
            pl.BlockSpec((1, heads, LENGTH), lambda s: (s, 0, 0)),
        ],
        out_shape=[
            jax.ShapeDtypeStruct((rows, cols), BF16),
            jax.ShapeDtypeStruct((sequences, heads, LENGTH), F32),
        ],
        scratch_shapes=[pltpu.VMEM((heads, LENGTH, LENGTH), F32)],
        compiler_params=pltpu.CompilerParams(
            dimension_semantics=("arbitrary",), vmem_limit_bytes=40 << 20
        ),
    )(rel, qkv)


def attend_back_kernel(
    rel_ref, qkv_ref, lse_ref, grad_ref, dqkv_ref, drel_ref, bias_ref, near_ref, *, heads
):
    tiles = LENGTH // TILE

    @pl.when(pl.program_id(0) == 0)
    def _():
        fill_bias(rel_ref, bias_ref, heads)
        near_ref[...] = jnp.zeros_like(near_ref)

    cols = heads * DH
    dqs, dks, dvs = [], [], []
    for h in range(heads):
        query = qkv_ref[:, h * DH : (h + 1) * DH]
        keys = qkv_ref[:, cols + h * DH : cols + (h + 1) * DH]
        values = qkv_ref[:, 2 * cols + h * DH : 2 * cols + (h + 1) * DH]
        grad = grad_ref[:, h * DH : (h + 1) * DH]
        scores = dot_right(keys, query) * 0.125 + bias_ref[h]
        probs = jnp.exp(scores - lse_ref[0, h : h + 1, :])
        dvs.append(dot(probs.astype(BF16), grad).astype(BF16))
        dprobs = dot_right(values, grad)
        weighted = jnp.sum(probs * dprobs, axis=0, keepdims=True)
        dscores = (probs * (dprobs - weighted)).astype(BF16)
        dks.append((dot(dscores, query) * 0.125).astype(BF16))
        dqs.append((dot_left(dscores, keys) * 0.125).astype(BF16))
        wide = dscores.astype(F32)
        sums = [None] * 5
        for i in range(tiles):
            for j in range(tiles):
                place = max(-2, min(2, i - j)) + 2
                block = wide[i * TILE : (i + 1) * TILE, j * TILE : (j + 1) * TILE]
                sums[place] = block if sums[place] is None else sums[place] + block
        for place in range(5):
            near_ref[h, place] = near_ref[h, place] + sums[place]
    dqkv_ref[...] = jnp.concatenate(dqs + dks + dvs, axis=1)

    @pl.when(pl.program_id(0) == pl.num_programs(0) - 1)
    def _():
        edges = STARTS + [1 << 20]
        for h in range(heads):
            rows = [jnp.zeros((1, TILE), F32) for _ in range(2 * HALF)]
            for delta in (-1, 0, 1):
                offset = offset_block(delta)
                block = near_ref[h, delta + 2]
                if delta == 0:
                    rows[0] = jnp.sum(
                        jnp.where(offset == 0, block, 0.0), axis=0, keepdims=True
                    )
                for step in range(HALF - 1):
                    if delta <= 0:
                        mask = (offset <= -edges[step]) & (offset > -edges[step + 1])
                        rows[step + 1] = rows[step + 1] + jnp.sum(
                            jnp.where(mask, block, 0.0), axis=0, keepdims=True
                        )
                    if delta >= 0:
                        mask = (offset >= edges[step]) & (offset < edges[step + 1])
                        rows[HALF + step + 1] = rows[HALF + step + 1] + jnp.sum(
                            jnp.where(mask, block, 0.0), axis=0, keepdims=True
                        )
            rows[HALF - 1] = rows[HALF - 1] + jnp.sum(near_ref[h, 0], axis=0, keepdims=True)
            rows[2 * HALF - 1] = rows[2 * HALF - 1] + jnp.sum(
                near_ref[h, 4], axis=0, keepdims=True
            )
            drel_ref[h] = jnp.concatenate(rows, axis=0)


def attend_back(qkv, rel, lse, grad):
    rows = qkv.shape[0]
    heads = rel.shape[1]
    cols = heads * DH
    sequences = rows // LENGTH
    return pl.pallas_call(
        functools.partial(attend_back_kernel, heads=heads),
        grid=(sequences,),
        in_specs=[
            pl.BlockSpec(memory_space=pltpu.SMEM),
            pl.BlockSpec((LENGTH, 3 * cols), lambda s: (s, 0)),
            pl.BlockSpec((1, heads, LENGTH), lambda s: (s, 0, 0)),
            pl.BlockSpec((LENGTH, cols), lambda s: (s, 0)),
        ],
        out_specs=[
            pl.BlockSpec((LENGTH, 3 * cols), lambda s: (s, 0)),
            pl.BlockSpec((heads, 2 * HALF, TILE), lambda s: (0, 0, 0)),
        ],
        out_shape=[
            jax.ShapeDtypeStruct((rows, 3 * cols), BF16),
            jax.ShapeDtypeStruct((heads, 2 * HALF, TILE), F32),
        ],
        scratch_shapes=[
            pltpu.VMEM((heads, LENGTH, LENGTH), F32),
            pltpu.VMEM((heads, 5, TILE, TILE), F32),
        ],
        compiler_params=pltpu.CompilerParams(
            dimension_semantics=("arbitrary",), vmem_limit_bytes=40 << 20
        ),
    )(rel, qkv, lse, grad)


def swap_tensor(block, distance):
    devices = lax.axis_size("tensor")
    return lax.ppermute(block, "tensor", [(i, i ^ distance) for i in range(devices)])


def gather_tensor(block):
    return [block] + [swap_tensor(block, d) for d in range(1, lax.axis_size("tensor"))]


def exchange_tensor(blocks):
    return [blocks[0]] + [swap_tensor(blocks[d], d) for d in range(1, len(blocks))]


def swap_section(block):
    return lax.ppermute(block, "section", [(0, 1), (1, 0)])


def swap_experts(block):
    return lax.all_to_all(block, "expert", split_axis=0, concat_axis=0, tiled=True)


def sum_blocks(blocks):
    total = blocks[0].astype(F32)
    for block in blocks[1:]:
        total = total + block.astype(F32)
    return total


def make_plan(route_rows, keep_rows, experts, capacity):
    tokens = route_rows.shape[0]
    devices = lax.axis_size("tensor")
    rank = lax.axis_index("tensor")
    owned = tokens // devices
    share = capacity // devices
    ids = jnp.arange(experts, dtype=jnp.int32)
    chosen = route_rows[:, None] == ids[None, :]
    order = jnp.arange(tokens, dtype=jnp.int32)
    lower = (order[:, None] > order[None, :]).astype(BF16)
    before = dot(lower, chosen.astype(BF16))
    chosen_f = chosen.astype(F32)
    counts = jnp.sum(chosen_f, axis=0)
    starts = jnp.sum(jnp.where(ids[None, :] < ids[:, None], counts[None, :], 0.0), axis=1)
    position = jnp.sum(chosen_f * (before + starts[None, :]), axis=1).astype(jnp.int32)
    distances = jnp.arange(devices, dtype=jnp.int32)
    rows = jnp.arange(owned, dtype=jnp.int32)
    wanted = (rows[None, :] * devices + (rank ^ distances)[:, None]).reshape(-1)
    deal = (wanted[:, None] == position[None, :]).astype(BF16)
    mine = wanted[:owned, None] == position[None, :]
    route_own = jnp.sum(jnp.where(mine, route_rows[None, :], 0), axis=1, dtype=jnp.int32)
    keep_own = jnp.sum(jnp.where(mine, keep_rows[None, :], 0), axis=1, dtype=jnp.int32)
    chosen_own = route_own[:, None] == ids[None, :]
    first = (starts.astype(jnp.int32) - rank + devices - 1) // devices
    slot = rows - jnp.sum(jnp.where(chosen_own, first[None, :], 0), axis=1, dtype=jnp.int32)
    slot = jnp.where(keep_own > 0, route_own * share + slot, -1)
    place = (jnp.arange(experts * share, dtype=jnp.int32)[:, None] == slot[None, :]).astype(BF16)
    return (deal, deal[:owned], place, chosen_own.astype(F32), keep_own.astype(F32))


def to_experts(rows, place, local):
    groups = lax.axis_size("expert")
    width = rows.shape[1]
    sent = dot(place, rows).astype(BF16).reshape(groups, -1, width)
    got = swap_experts(sent)
    share = got.shape[1] // local
    got = got.reshape(groups, local, share, width).transpose(1, 0, 2, 3)
    got = got.reshape(local, groups * share, width)
    return jnp.concatenate(gather_tensor(got), axis=1)


def from_experts(parts, place):
    groups = lax.axis_size("expert")
    devices = lax.axis_size("tensor")
    local, slots, width = parts.shape
    own = slots // devices
    parts = parts.astype(BF16)
    blocks = exchange_tensor([parts[:, d * own : (d + 1) * own] for d in range(devices)])
    summed = sum_blocks(blocks).astype(BF16)
    summed = summed.reshape(local, groups, own // groups, width).transpose(1, 0, 2, 3)
    back = swap_experts(summed.reshape(groups, -1, width)).reshape(-1, width)
    return dot_left(place, back)


def per_expert(left, right, contract):
    return lax.dot_general(
        left, right, ((contract[:1], contract[1:]), ((0,), (0,))), preferred_element_type=F32
    )


def layer_forward(rows_in, weights, rel, plan):
    attn_gain, ffn_gain, w_qkv, w_out, w_router, w_in, w_back = weights
    deal, deal_own, place, chosen, kept = plan
    devices = lax.axis_size("tensor")
    local = w_in.shape[0]
    layer_in = rows_in.astype(F32)
    scale_one = root_mean(layer_in)
    normed = (layer_in * scale_one * attn_gain).astype(BF16)
    qkv = dot(normed, w_qkv).astype(BF16)
    mixed, lse = attend(qkv, rel)
    cols = mixed.shape[1]
    dealt = dot(deal, mixed).astype(BF16).reshape(devices, -1, cols)
    heads = exchange_tensor([dealt[d] for d in range(devices)])
    own_in = dot(deal_own, rows_in)
    branch = sum(dot(heads[d], w_out[d]) for d in range(devices))
    middle = own_in + branch
    scale_two = root_mean(middle)
    normed_two = (middle * scale_two * ffn_gain).astype(BF16)
    probs = jax.nn.softmax(dot(normed_two, w_router), axis=-1)
    gate = jnp.sum(probs * chosen, axis=-1)
    incoming = to_experts(normed_two, place, local)
    inner = per_expert(incoming, w_in, (2, 1))
    cumulative = 0.5 * (1.0 + lax.erf(inner * np.float32(np.sqrt(0.5))))
    density = jnp.exp(-0.5 * inner * inner) * np.float32(1.0 / np.sqrt(2.0 * np.pi))
    hidden = (inner * cumulative).astype(BF16)
    slope = (cumulative + inner * density).astype(BF16)
    per_token = from_experts(per_expert(hidden, w_back, (2, 1)), place)
    output = (middle + (kept * gate)[:, None] * per_token).astype(BF16)
    every = jnp.concatenate(gather_tensor(output), axis=0)
    rows_out = dot_left(deal, every).astype(BF16)
    saved = (own_in, normed, qkv, lse, heads, middle, normed_two, probs, gate)
    return (rows_out, saved + (incoming, hidden, slope, per_token))


def norm_back(grad, values, gain):
    scale = root_mean(values)
    scaled = grad * gain
    values_grad = scale * scaled - values * (scale * scale * scale) * jnp.mean(
        scaled * values, axis=-1, keepdims=True
    )
    return (values_grad, jnp.sum(grad * values * scale, axis=0))


def layer_backward(saved, rows_grad, weights, rel, plan):
    attn_gain, ffn_gain, w_qkv, w_out, w_router, w_in, w_back = weights
    deal, deal_own, place, chosen, kept = plan
    own_in, normed, qkv, lse, heads, middle, normed_two, probs, gate = saved[:9]
    incoming, hidden, slope, per_token = saved[9:]
    devices = lax.axis_size("tensor")
    local = w_in.shape[0]
    grad_out = dot(deal_own, rows_grad)
    gated = ((kept * gate)[:, None] * grad_out).astype(BF16)
    gate_grad = kept * jnp.sum(grad_out * per_token, axis=-1)
    expert_grad = to_experts(gated, place, local)
    hidden_grad = per_expert(expert_grad, w_back, (2, 2))
    inner_grad = (hidden_grad * slope.astype(F32)).astype(BF16)
    input_rows = from_experts(per_expert(inner_grad, w_in, (2, 2)), place)
    back_grad = per_expert(hidden, expert_grad, (1, 1))
    in_grad = per_expert(incoming, inner_grad, (1, 1))
    logit_grad = (probs * (chosen - gate[:, None]) * gate_grad[:, None]).astype(BF16)
    router_grad = dot_left(normed_two, logit_grad)
    normed_two_grad = input_rows + dot_right(logit_grad, w_router)
    middle_part, ffn_grad = norm_back(normed_two_grad, middle, ffn_gain)
    middle_grad = grad_out + middle_part
    branch_grad = middle_grad.astype(BF16)
    head_grads = exchange_tensor(
        [dot_right(branch_grad, w_out[d]).astype(BF16) for d in range(devices)]
    )
    mixed_grad = dot_left(deal, jnp.concatenate(head_grads, axis=0)).astype(BF16)
    out_grad = jnp.stack([dot_left(heads[d], branch_grad) for d in range(devices)])
    dqkv, drel = attend_back(qkv, rel, lse, mixed_grad)
    normed_parts = dot_right(dot(deal, dqkv).astype(BF16), w_qkv).astype(BF16)
    normed_parts = normed_parts.reshape(devices, -1, normed_parts.shape[1])
    normed_grad = sum_blocks(exchange_tensor([normed_parts[d] for d in range(devices)]))
    layer_part, attn_grad = norm_back(normed_grad, own_in, attn_gain)
    layer_grad = (middle_grad + layer_part).astype(BF16)
    every = jnp.concatenate(gather_tensor(layer_grad), axis=0)
    rows_out = dot_left(deal, every).astype(BF16)
    qkv_grad = dot_left(normed, dqkv)
    rel_grad = jnp.sum(drel, axis=-1).T
    small = jnp.concatenate([attn_grad[None], ffn_grad[None], router_grad.T], axis=0)
    return (rows_out, (qkv_grad, out_grad, small, rel_grad, in_grad, back_grad))


def body(
    x_in,
    cotangent,
    attn_gain,
    ffn_gain,
    w_query,
    w_key,
    w_value,
    w_out,
    rel_bias,
    w_router,
    w_in,
    w_back,
    routes,
    keep_mask,
):
    core = lax.axis_index("section")
    first = core == 0
    groups = lax.axis_size("expert")
    devices = lax.axis_size("tensor")
    experts = w_router.shape[2]
    tokens = x_in.shape[1]
    width = x_in.shape[2]
    capacity = 3 * tokens // (2 * experts)

    def both(own):
        other = swap_section(own)
        return (jnp.where(first, own, other), jnp.where(first, other, own))

    def pick(stack, index):
        return lax.dynamic_index_in_dim(stack, index, 0, keepdims=False)

    qkv_pair = both(jnp.concatenate([w_query[0], w_key[0], w_value[0]], axis=1))
    rel_pair = both(rel_bias[0])
    attn_pair = both(attn_gain)
    ffn_pair = both(ffn_gain)
    router_pair = both(w_router[0])
    out_pair = both(jnp.stack(gather_tensor(w_out[0])))
    in_all = lax.all_gather(w_in[0], "section", axis=0)
    back_all = lax.all_gather(w_back[0], "section", axis=0)
    own_ints = jnp.stack([pick(routes[0], core)[:, 0], pick(keep_mask[0], core)])
    sent_ints = jnp.stack([pick(routes[0], 1 - core)[:, 0], pick(keep_mask[0], 1 - core)])
    got_ints = swap_section(sent_ints)
    ints_pair = (jnp.where(first, own_ints, got_ints), jnp.where(first, got_ints, own_ints))

    weights, rels, plans = [], [], []
    for s in range(2):
        weights.append(
            (
                attn_pair[s][0].astype(F32),
                ffn_pair[s][0].astype(F32),
                qkv_pair[s],
                out_pair[s],
                router_pair[s],
                in_all[s],
                back_all[s],
            )
        )
        rels.append(rel_pair[s].astype(F32))
        plans.append(make_plan(ints_pair[s][0], ints_pair[s][1], experts, capacity))

    rows = pick(x_in, core)
    acts, saved = [], []
    for s in range(2):
        rows, kept = layer_forward(rows, weights[s], rels[s], plans[s])
        acts.append(rows)
        saved.append(kept)
    grads = [None, None]
    row_grads = [None, None]
    rows = pick(cotangent, core)
    for s in (1, 0):
        rows, grads[s] = layer_backward(saved[s], rows, weights[s], rels[s], plans[s])
        row_grads[s] = rows

    def whole_rows(pair):
        own = jnp.where(first, pair[0], pair[1])
        got = swap_section(jnp.where(first, pair[1], pair[0]))
        return jnp.stack([jnp.where(first, own, got), jnp.where(first, got, own)])[None]

    def whole_grad(number):
        low, high = grads[0][number], grads[1][number]
        got = swap_section(jnp.where(first, high, low).astype(BF16))
        return jnp.where(first, low, high) + got.astype(F32)

    qkv_grad, out_grad, small, rel_grad, in_grad, back_grad = [whole_grad(n) for n in range(6)]
    tall = jnp.concatenate(
        [out_grad, jnp.broadcast_to(small[None], (devices,) + small.shape)], axis=1
    ).astype(BF16)
    tall = sum_blocks(exchange_tensor([tall[d] for d in range(devices)]))
    wide = jnp.concatenate([qkv_grad, tall.T], axis=1)
    rel_wide = jnp.pad(rel_grad, ((0, 0), (0, wide.shape[1] - rel_grad.shape[1])))
    packed = jnp.concatenate(
        [wide.reshape(groups, -1, wide.shape[1]), rel_wide.reshape(groups, -1, wide.shape[1])],
        axis=1,
    ).astype(BF16)
    shares = jnp.sum(swap_experts(packed).astype(F32), axis=0)
    mine = width // groups
    cols = w_query.shape[2]
    return (
        whole_rows(acts),
        whole_rows(row_grads),
        shares[:mine, 4 * cols][None],
        shares[:mine, 4 * cols + 1][None],
        shares[:mine, :cols][None],
        shares[:mine, cols : 2 * cols][None],
        shares[:mine, 2 * cols : 3 * cols][None],
        shares[:mine, 3 * cols : 4 * cols].T[None],
        shares[mine:, : rel_bias.shape[2]][None],
        shares[:mine, 4 * cols + 2 :][None],
        in_grad[None],
        back_grad[None],
    )


def solution(mesh):
    placed = (
        P(None, "expert", None),
        P(None, "expert", None),
        P("section", None),
        P("section", None),
        P("section", None, "tensor"),
        P("section", None, "tensor"),
        P("section", None, "tensor"),
        P("section", "tensor", None),
        P("section", None, "tensor"),
        P("section", None, None),
        P("section", "expert", None, "tensor"),
        P("section", "expert", "tensor", None),
        P("section", None, "expert", None),
        P("section", None, "expert"),
    )
    return jax.shard_map(
        body,
        mesh=mesh,
        in_specs=placed,
        out_specs=(
            P("section", None, "expert", None),
            P("section", None, "expert", None),
            P("section", "expert"),
            P("section", "expert"),
            P("section", "expert", "tensor"),
            P("section", "expert", "tensor"),
            P("section", "expert", "tensor"),
            P("section", "tensor", "expert"),
            P("section", "expert", "tensor"),
            P("section", "expert", None),
            P("section", "expert", None, "tensor"),
            P("section", "expert", "tensor", None),
        ),
        check_vma=False,
    )
```

```python
import functools
import jax
import jax.numpy as jnp
import numpy as np
from jax import lax
from jax.experimental import pallas as pl
from jax.experimental.pallas import tpu as pltpu
from jax.sharding import PartitionSpec as P

DH = 64
LENGTH = 512
TILE = 128
EPSILON = 1e-06
BF16 = jnp.bfloat16
F32 = jnp.float32


def bucket_starts():
    starts = list(range(1, 9))
    for ladder in range(1, 8):
        distance = 8
        while distance**8 < 2 ** (24 + 4 * ladder):
            distance = distance + 1
        starts.append(distance)
    return starts


STARTS = bucket_starts()
HALF = len(STARTS) + 1


def root_mean(values):
    return lax.rsqrt(jnp.mean(values * values, axis=-1, keepdims=True) + EPSILON)


def dot(left, right):
    return jnp.dot(left, right, preferred_element_type=F32)


def dot_left(left, right):
    return lax.dot_general(left, right, (((0,), (0,)), ((), ())), preferred_element_type=F32)


def dot_right(left, right):
    return lax.dot_general(left, right, (((1,), (1,)), ((), ())), preferred_element_type=F32)


def offset_block(delta):
    rows = lax.broadcasted_iota(jnp.int32, (TILE, TILE), 0)
    cols = lax.broadcasted_iota(jnp.int32, (TILE, TILE), 1)
    return rows - cols + delta * TILE


def fill_bias(rel_ref, bias_ref, heads):
    tiles = LENGTH // TILE
    for delta in (-1, 0, 1):
        offset = offset_block(delta)
        blocks = [jnp.full((TILE, TILE), rel_ref[0, h], F32) for h in range(heads)]
        for step, start in enumerate(STARTS):
            if delta <= 0:
                mask = offset <= -start
                blocks = [
                    jnp.where(mask, rel_ref[step + 1, h], block) for h, block in enumerate(blocks)
                ]
            if delta >= 0:
                mask = offset >= start
                blocks = [
                    jnp.where(mask, rel_ref[HALF + step + 1, h], block)
                    for h, block in enumerate(blocks)
                ]
        for h in range(heads):
            for i in range(tiles):
                j = i - delta
                if 0 <= j < tiles:
                    bias_ref[h, i * TILE : (i + 1) * TILE, j * TILE : (j + 1) * TILE] = blocks[h]
    for h in range(heads):
        above = jnp.full((TILE, TILE), rel_ref[2 * HALF - 1, h], F32)
        below = jnp.full((TILE, TILE), rel_ref[HALF - 1, h], F32)
        for i in range(tiles):
            for j in range(tiles):
                if abs(i - j) > 1:
                    bias_ref[h, i * TILE : (i + 1) * TILE, j * TILE : (j + 1) * TILE] = (
                        above if i > j else below
                    )


def attend_kernel(rel_ref, qkv_ref, mixed_ref, lse_ref, bias_ref, *, heads):
    @pl.when(pl.program_id(0) == 0)
    def _():
        fill_bias(rel_ref, bias_ref, heads)

    cols = heads * DH
    outs = []
    for h in range(heads):
        query = qkv_ref[:, h * DH : (h + 1) * DH]
        keys = qkv_ref[:, cols + h * DH : cols + (h + 1) * DH]
        values = qkv_ref[:, 2 * cols + h * DH : 2 * cols + (h + 1) * DH]
        scores = dot_right(keys, query) * 0.125 + bias_ref[h]
        highest = jnp.max(scores, axis=0, keepdims=True)
        raised = jnp.exp(scores - highest)
        total = jnp.sum(raised, axis=0, keepdims=True)
        probs = (raised * (1.0 / total)).astype(BF16)
        outs.append(dot_left(probs, values).astype(BF16))
        lse_ref[0, h : h + 1, :] = highest + jnp.log(total)
    mixed_ref[...] = jnp.concatenate(outs, axis=1)


def attend(qkv, rel):
    rows = qkv.shape[0]
    heads = rel.shape[1]
    cols = heads * DH
    sequences = rows // LENGTH
    return pl.pallas_call(
        functools.partial(attend_kernel, heads=heads),
        grid=(sequences,),
        in_specs=[
            pl.BlockSpec(memory_space=pltpu.SMEM),
            pl.BlockSpec((LENGTH, 3 * cols), lambda s: (s, 0)),
        ],
        out_specs=[
            pl.BlockSpec((LENGTH, cols), lambda s: (s, 0)),
            pl.BlockSpec((1, heads, LENGTH), lambda s: (s, 0, 0)),
        ],
        out_shape=[
            jax.ShapeDtypeStruct((rows, cols), BF16),
            jax.ShapeDtypeStruct((sequences, heads, LENGTH), F32),
        ],
        scratch_shapes=[pltpu.VMEM((heads, LENGTH, LENGTH), F32)],
        compiler_params=pltpu.CompilerParams(
            dimension_semantics=("arbitrary",), vmem_limit_bytes=40 << 20
        ),
    )(rel, qkv)


def attend_back_kernel(
    rel_ref, qkv_ref, lse_ref, grad_ref, dqkv_ref, drel_ref, bias_ref, near_ref, *, heads
):
    tiles = LENGTH // TILE

    @pl.when(pl.program_id(0) == 0)
    def _():
        fill_bias(rel_ref, bias_ref, heads)
        near_ref[...] = jnp.zeros_like(near_ref)

    cols = heads * DH
    dqs, dks, dvs = [], [], []
    for h in range(heads):
        query = qkv_ref[:, h * DH : (h + 1) * DH]
        keys = qkv_ref[:, cols + h * DH : cols + (h + 1) * DH]
        values = qkv_ref[:, 2 * cols + h * DH : 2 * cols + (h + 1) * DH]
        grad = grad_ref[:, h * DH : (h + 1) * DH]
        scores = dot_right(keys, query) * 0.125 + bias_ref[h]
        probs = jnp.exp(scores - lse_ref[0, h : h + 1, :])
        dvs.append(dot(probs.astype(BF16), grad).astype(BF16))
        dprobs = dot_right(values, grad)
        weighted = jnp.sum(probs * dprobs, axis=0, keepdims=True)
        dscores = (probs * (dprobs - weighted)).astype(BF16)
        dks.append((dot(dscores, query) * 0.125).astype(BF16))
        dqs.append((dot_left(dscores, keys) * 0.125).astype(BF16))
        wide = dscores.astype(F32)
        sums = [None] * 5
        for i in range(tiles):
            for j in range(tiles):
                place = max(-2, min(2, i - j)) + 2
                block = wide[i * TILE : (i + 1) * TILE, j * TILE : (j + 1) * TILE]
                sums[place] = block if sums[place] is None else sums[place] + block
        for place in range(5):
            near_ref[h, place] = near_ref[h, place] + sums[place]
    dqkv_ref[...] = jnp.concatenate(dqs + dks + dvs, axis=1)

    @pl.when(pl.program_id(0) == pl.num_programs(0) - 1)
    def _():
        edges = STARTS + [1 << 20]
        for h in range(heads):
            rows = [jnp.zeros((1, TILE), F32) for _ in range(2 * HALF)]
            for delta in (-1, 0, 1):
                offset = offset_block(delta)
                block = near_ref[h, delta + 2]
                if delta == 0:
                    rows[0] = jnp.sum(
                        jnp.where(offset == 0, block, 0.0), axis=0, keepdims=True
                    )
                for step in range(HALF - 1):
                    if delta <= 0:
                        mask = (offset <= -edges[step]) & (offset > -edges[step + 1])
                        rows[step + 1] = rows[step + 1] + jnp.sum(
                            jnp.where(mask, block, 0.0), axis=0, keepdims=True
                        )
                    if delta >= 0:
                        mask = (offset >= edges[step]) & (offset < edges[step + 1])
                        rows[HALF + step + 1] = rows[HALF + step + 1] + jnp.sum(
                            jnp.where(mask, block, 0.0), axis=0, keepdims=True
                        )
            rows[HALF - 1] = rows[HALF - 1] + jnp.sum(near_ref[h, 0], axis=0, keepdims=True)
            rows[2 * HALF - 1] = rows[2 * HALF - 1] + jnp.sum(
                near_ref[h, 4], axis=0, keepdims=True
            )
            drel_ref[h] = jnp.concatenate(rows, axis=0)


def attend_back(qkv, rel, lse, grad):
    rows = qkv.shape[0]
    heads = rel.shape[1]
    cols = heads * DH
    sequences = rows // LENGTH
    return pl.pallas_call(
        functools.partial(attend_back_kernel, heads=heads),
        grid=(sequences,),
        in_specs=[
            pl.BlockSpec(memory_space=pltpu.SMEM),
            pl.BlockSpec((LENGTH, 3 * cols), lambda s: (s, 0)),
            pl.BlockSpec((1, heads, LENGTH), lambda s: (s, 0, 0)),
            pl.BlockSpec((LENGTH, cols), lambda s: (s, 0)),
        ],
        out_specs=[
            pl.BlockSpec((LENGTH, 3 * cols), lambda s: (s, 0)),
            pl.BlockSpec((heads, 2 * HALF, TILE), lambda s: (0, 0, 0)),
        ],
        out_shape=[
            jax.ShapeDtypeStruct((rows, 3 * cols), BF16),
            jax.ShapeDtypeStruct((heads, 2 * HALF, TILE), F32),
        ],
        scratch_shapes=[
            pltpu.VMEM((heads, LENGTH, LENGTH), F32),
            pltpu.VMEM((heads, 5, TILE, TILE), F32),
        ],
        compiler_params=pltpu.CompilerParams(
            dimension_semantics=("arbitrary",), vmem_limit_bytes=40 << 20
        ),
    )(rel, qkv, lse, grad)


def swap_tensor(block, distance):
    devices = lax.axis_size("tensor")
    return lax.ppermute(block, "tensor", [(i, i ^ distance) for i in range(devices)])


def gather_tensor(block):
    return [block] + [swap_tensor(block, d) for d in range(1, lax.axis_size("tensor"))]


def exchange_tensor(blocks):
    return [blocks[0]] + [swap_tensor(blocks[d], d) for d in range(1, len(blocks))]


def swap_section(block):
    return lax.ppermute(block, "section", [(0, 1), (1, 0)])


def swap_experts(block):
    return lax.all_to_all(block, "expert", split_axis=0, concat_axis=0, tiled=True)


def sum_blocks(blocks):
    total = blocks[0].astype(F32)
    for block in blocks[1:]:
        total = total + block.astype(F32)
    return total


def chunks_of(local):
    return 2 if local % 2 == 0 else 1


def make_plan(route_rows, keep_rows, experts, capacity):
    tokens = route_rows.shape[0]
    devices = lax.axis_size("tensor")
    rank = lax.axis_index("tensor")
    owned = tokens // devices
    share = capacity // devices
    ids = jnp.arange(experts, dtype=jnp.int32)
    chosen = route_rows[:, None] == ids[None, :]
    order = jnp.arange(tokens, dtype=jnp.int32)
    lower = (order[:, None] > order[None, :]).astype(BF16)
    before = dot(lower, chosen.astype(BF16))
    chosen_f = chosen.astype(F32)
    counts = jnp.sum(chosen_f, axis=0)
    starts = jnp.sum(jnp.where(ids[None, :] < ids[:, None], counts[None, :], 0.0), axis=1)
    position = jnp.sum(chosen_f * (before + starts[None, :]), axis=1).astype(jnp.int32)
    distances = jnp.arange(devices, dtype=jnp.int32)
    rows = jnp.arange(owned, dtype=jnp.int32)
    wanted = (rows[None, :] * devices + (rank ^ distances)[:, None]).reshape(-1)
    deal = (wanted[:, None] == position[None, :]).astype(BF16)
    mine = wanted[:owned, None] == position[None, :]
    route_own = jnp.sum(jnp.where(mine, route_rows[None, :], 0), axis=1, dtype=jnp.int32)
    keep_own = jnp.sum(jnp.where(mine, keep_rows[None, :], 0), axis=1, dtype=jnp.int32)
    chosen_own = route_own[:, None] == ids[None, :]
    first = (starts.astype(jnp.int32) - rank + devices - 1) // devices
    slot = rows - jnp.sum(jnp.where(chosen_own, first[None, :], 0), axis=1, dtype=jnp.int32)
    slot = jnp.where(keep_own > 0, route_own * share + slot, -1)
    groups = lax.axis_size("expert")
    local = experts // groups
    chunks = chunks_of(local)
    ahead = (lax.axis_index("expert") + jnp.arange(groups, dtype=jnp.int32)) % groups
    inner = np.arange(local * share, dtype=np.int32).reshape(chunks, -1)
    places = []
    for chunk in inner:
        wanted_slot = (ahead[:, None] * (local * share) + chunk[None, :]).reshape(-1)
        places.append((wanted_slot[:, None] == slot[None, :]).astype(BF16))
    return (deal, deal[:owned], places, chosen_own.astype(F32), keep_own.astype(F32))


def shift_experts(block, distance):
    groups = lax.axis_size("expert")
    if distance % groups == 0:
        return block
    return lax.ppermute(block, "expert", [(i, (i + distance) % groups) for i in range(groups)])


def to_groups(rows, local):
    groups = lax.axis_size("expert")
    rows = rows.reshape(groups, local, -1, rows.shape[1])
    return jnp.concatenate([shift_experts(rows[d], d) for d in range(groups)], axis=1)


def all_shares(got):
    return jnp.concatenate(gather_tensor(got), axis=1)


def send_tokens(rows, places, local):
    per_chunk = local // len(places)
    return [to_groups(dot(place, rows).astype(BF16), per_chunk) for place in places]


def from_experts(parts, place):
    groups = lax.axis_size("expert")
    devices = lax.axis_size("tensor")
    local, slots, width = parts.shape
    own = slots // devices
    parts = parts.astype(BF16)
    blocks = exchange_tensor([parts[:, d * own : (d + 1) * own] for d in range(devices)])
    summed = sum_blocks(blocks).astype(BF16)
    share = own // groups
    back = [
        shift_experts(summed[:, d * share : (d + 1) * share].reshape(-1, width), -d)
        for d in range(groups)
    ]
    return dot_left(place, jnp.concatenate(back, axis=0))


def per_expert(left, right, contract):
    return lax.dot_general(
        left, right, ((contract[:1], contract[1:]), ((0,), (0,))), preferred_element_type=F32
    )


def grads_kernel(pick_ref, *refs, chunks, per_chunk):
    lefts, rights = refs[: 2 * chunks], refs[2 * chunks : 4 * chunks]
    extra, out_ref = refs[4 * chunks : -1], refs[-1]
    expert = pl.program_id(0)
    for layer in range(2):
        for c in range(chunks):

            @pl.when((pick_ref[0] == layer) & (expert // per_chunk == c))
            def _():
                value = dot_left(lefts[layer * chunks + c][0], rights[layer * chunks + c][0])
                for ref in extra:
                    value = value + ref[0].astype(F32)
                out_ref[0] = value.astype(out_ref.dtype)


def expert_grads(lefts, rights, layer, extra, kind):
    chunks = len(lefts[0])
    per_chunk, slots, rows = lefts[0][0].shape
    cols = rights[0][0].shape[2]
    local = chunks * per_chunk

    def spec(owner, c, width):
        def place(e, pick):
            own = jnp.clip(e - c * per_chunk, 0, per_chunk - 1)
            return (jnp.where(pick[0] == owner, own, 0), 0, 0)

        return pl.BlockSpec((1, slots, width), place)

    whole = pl.BlockSpec((1, rows, cols), lambda e, pick: (e, 0, 0))
    names = [(owner, c) for owner in range(2) for c in range(chunks)]
    return pl.pallas_call(
        functools.partial(grads_kernel, chunks=chunks, per_chunk=per_chunk),
        grid_spec=pltpu.PrefetchScalarGridSpec(
            num_scalar_prefetch=1,
            grid=(local,),
            in_specs=[spec(owner, c, rows) for owner, c in names]
            + [spec(owner, c, cols) for owner, c in names]
            + [whole] * len(extra),
            out_specs=whole,
        ),
        out_shape=jax.ShapeDtypeStruct((local, rows, cols), kind),
        compiler_params=pltpu.CompilerParams(
            dimension_semantics=("arbitrary",), vmem_limit_bytes=40 << 20
        ),
        cost_estimate=pl.CostEstimate(
            flops=2 * local * slots * rows * cols,
            transcendentals=0,
            bytes_accessed=local * (6 * rows * cols + 2 * slots * (rows + cols)),
        ),
    )(layer, *lefts[0], *lefts[1], *rights[0], *rights[1], *extra)


def layer_forward(rows_in, weights, rel, plan, ahead, with_gates):
    attn_gain, ffn_gain, w_qkv, w_out, w_router, w_in, w_back = weights
    deal, deal_own, places, chosen, kept = plan
    devices = lax.axis_size("tensor")
    local = sum(block.shape[0] for block in w_in)
    layer_in = rows_in.astype(F32)
    scale_one = root_mean(layer_in)
    normed = (layer_in * scale_one * attn_gain).astype(BF16)
    qkv = dot(normed, w_qkv).astype(BF16)
    mixed, lse = attend(qkv, rel)
    if with_gates:
        mixed, ahead = lax.optimization_barrier((mixed, ahead))
    cols = mixed.shape[1]
    dealt = dot(deal, mixed).astype(BF16).reshape(devices, -1, cols)
    heads = exchange_tensor([dealt[d] for d in range(devices)])
    own_in = dot(deal_own, rows_in)
    branch = sum(dot(heads[d], w_out[d]) for d in range(devices))
    middle = own_in + branch
    scale_two = root_mean(middle)
    normed_two = (middle * scale_two * ffn_gain).astype(BF16)
    probs = jax.nn.softmax(dot(normed_two, w_router), axis=-1)
    gate = jnp.sum(probs * chosen, axis=-1)
    gates = send_gates(kept * gate, places, local) if with_gates else None
    incoming = [all_shares(got) for got in send_tokens(normed_two, places, local)]
    if not with_gates:
        incoming[-1], ahead = lax.optimization_barrier((incoming[-1], ahead))
    hidden, slope, per_token = [], [], 0.0
    for place, rows, first, second in zip(places, incoming, w_in, w_back):
        inner = per_expert(rows, first, (2, 1))
        cumulative = 0.5 * (1.0 + lax.erf(inner * np.float32(np.sqrt(0.5))))
        density = jnp.exp(-0.5 * inner * inner) * np.float32(1.0 / np.sqrt(2.0 * np.pi))
        hidden.append((inner * cumulative).astype(BF16))
        slope.append((cumulative + inner * density).astype(BF16))
        parts = per_expert(hidden[-1], second, (2, 1)).astype(BF16)
        if with_gates:
            parts, gates = lax.optimization_barrier((parts, gates))
        per_token = per_token + from_experts(parts, place)
    output = (middle + (kept * gate)[:, None] * per_token).astype(BF16)
    every = jnp.concatenate(gather_tensor(output), axis=0)
    rows_out = dot_left(deal, every).astype(BF16)
    saved = (own_in, normed, qkv, lse, heads, middle, normed_two, probs, gate)
    return (rows_out, saved + (incoming, hidden, slope, per_token), ahead, gates)


def norm_back(grad, values, gain):
    scale = root_mean(values)
    scaled = grad * gain
    values_grad = scale * scaled - values * (scale * scale * scale) * jnp.mean(
        scaled * values, axis=-1, keepdims=True
    )
    return (values_grad, jnp.sum(grad * values * scale, axis=0))


def send_gates(gates, places, local):
    groups = lax.axis_size("expert")
    factors = [
        jnp.sum(place.astype(F32) * gates[None, :], axis=1).reshape(groups, local // len(places), -1)
        for place in places
    ]
    factors = jnp.concatenate(factors, axis=1)
    got = jnp.concatenate([shift_experts(factors[d], d) for d in range(groups)], axis=1)
    return jnp.split(all_shares(got)[:, :, None], len(places))


def layer_backward(saved, rows_grad, weights, rel, plan, early, gates, finish):
    attn_gain, ffn_gain, w_qkv, w_out, w_router, w_in, w_back = weights
    deal, deal_own, places, chosen, kept = plan
    own_in, normed, qkv, lse, heads, middle, normed_two, probs, gate = saved[:9]
    incoming, hidden, slope, per_token = saved[9:]
    devices = lax.axis_size("tensor")
    local = sum(block.shape[0] for block in w_in)
    grad_out = dot(deal_own, rows_grad)
    gated = ((kept * gate)[:, None] * grad_out).astype(BF16)
    gate_grad = kept * jnp.sum(grad_out * per_token, axis=-1)
    if early is None:
        expert_grad = [all_shares(got) for got in send_tokens(gated, places, local)]
    else:
        expert_grad = [
            (factor * rows.astype(F32)).astype(BF16) for factor, rows in zip(gates, early)
        ]
    input_rows, inner_grads = 0.0, []
    for n, place in enumerate(places):
        hidden_grad = per_expert(expert_grad[n], w_back[n], (2, 2))
        inner_grad = (hidden_grad * slope[n].astype(F32)).astype(BF16)
        input_rows = input_rows + from_experts(per_expert(inner_grad, w_in[n], (2, 2)), place)
        inner_grads.append(inner_grad)
    logit_grad = (probs * (chosen - gate[:, None]) * gate_grad[:, None]).astype(BF16)
    router_grad = dot_left(normed_two, logit_grad)
    normed_two_grad = input_rows + dot_right(logit_grad, w_router)
    middle_part, ffn_grad = norm_back(normed_two_grad, middle, ffn_gain)
    middle_grad = grad_out + middle_part
    branch_grad = middle_grad.astype(BF16)
    head_grads = exchange_tensor(
        [dot_right(branch_grad, w_out[d]).astype(BF16) for d in range(devices)]
    )
    mixed_grad = dot_left(deal, jnp.concatenate(head_grads, axis=0)).astype(BF16)
    out_grad = jnp.stack([dot_left(heads[d], branch_grad) for d in range(devices)])
    small = jnp.concatenate([ffn_grad[None], router_grad.T], axis=0)
    beside, fill = finish[0](inner_grads, expert_grad, out_grad, small)
    dqkv, drel = attend_back(qkv, rel, lse, mixed_grad)
    dqkv, beside = lax.optimization_barrier((dqkv, beside))
    qkv_grad = dot_left(normed, dqkv)
    rel_grad = jnp.sum(drel, axis=-1).T
    normed_parts = dot_right(dot(deal, dqkv).astype(BF16), w_qkv).astype(BF16)
    normed_parts = normed_parts.reshape(devices, -1, normed_parts.shape[1])
    blocks = exchange_tensor([normed_parts[d] for d in range(devices)])
    blocks, fill = lax.optimization_barrier((blocks, fill))
    normed_grad = sum_blocks(blocks)
    layer_part, attn_grad = norm_back(normed_grad, own_in, attn_gain)
    layer_grad = (middle_grad + layer_part).astype(BF16)
    last = finish[1](qkv_grad, rel_grad, beside)
    blocks, last = lax.optimization_barrier((gather_tensor(layer_grad), last))
    rows_out = dot_left(deal, jnp.concatenate(blocks, axis=0)).astype(BF16)
    return (rows_out, (attn_grad, fill, last))


def body(
    x_in,
    cotangent,
    attn_gain,
    ffn_gain,
    w_query,
    w_key,
    w_value,
    w_out,
    rel_bias,
    w_router,
    w_in,
    w_back,
    routes,
    keep_mask,
):
    core = lax.axis_index("section")
    first = core == 0
    groups = lax.axis_size("expert")
    devices = lax.axis_size("tensor")
    experts = w_router.shape[2]
    tokens = x_in.shape[1]
    width = x_in.shape[2]
    capacity = 3 * tokens // (2 * experts)

    def both(own):
        other = swap_section(own)
        return (jnp.where(first, own, other), jnp.where(first, other, own))

    def pick(stack, index):
        return lax.dynamic_index_in_dim(stack, index, 0, keepdims=False)

    qkv_pair = both(jnp.concatenate([w_query[0], w_key[0], w_value[0]], axis=1))
    rel_pair = both(rel_bias[0])
    attn_pair = both(attn_gain)
    ffn_pair = both(ffn_gain)
    router_pair = both(w_router[0])
    out_pair = both(jnp.stack(gather_tensor(w_out[0])))
    in_all = lax.all_gather(w_in[0], "section", axis=0)
    back_all = lax.all_gather(w_back[0], "section", axis=0)
    own_ints = jnp.stack([pick(routes[0], core)[:, 0], pick(keep_mask[0], core)])
    sent_ints = jnp.stack([pick(routes[0], 1 - core)[:, 0], pick(keep_mask[0], 1 - core)])
    got_ints = swap_section(sent_ints)
    ints_pair = (jnp.where(first, own_ints, got_ints), jnp.where(first, got_ints, own_ints))

    chunks = chunks_of(w_in.shape[1])
    weights, rels, plans = [], [], []
    for s in range(2):
        weights.append(
            (
                attn_pair[s][0].astype(F32),
                ffn_pair[s][0].astype(F32),
                qkv_pair[s],
                out_pair[s],
                router_pair[s],
                jnp.split(in_all[s], chunks),
                jnp.split(back_all[s], chunks),
            )
        )
        rels.append(rel_pair[s].astype(F32))
        plans.append(make_plan(ints_pair[s][0], ints_pair[s][1], experts, capacity))

    ahead = send_tokens(
        dot(plans[1][1], pick(cotangent, core)).astype(BF16), plans[1][2], w_in.shape[1]
    )
    rows = pick(x_in, core)
    acts, saved = [], []
    for s in range(2):
        rows, kept, ahead, gates = layer_forward(rows, weights[s], rels[s], plans[s], ahead, s == 1)
        if s == 0:
            ahead = [all_shares(got) for got in ahead]
        acts.append(rows)
        saved.append(kept)
    def whole_grad(low, high):
        got = swap_section(jnp.where(first, high, low).astype(BF16))
        return jnp.where(first, low, high) + got.astype(F32)

    own_layer = core.reshape(1)
    mine = width // groups
    cols = w_query.shape[2]
    held_experts, held_attention = [], []

    def expert_part(inner_grads, expert_grad, out_grad, small):
        held = held_experts
        held.append((inner_grads, expert_grad, out_grad, small))
        if len(held) < 2:
            return ((out_grad, small), ())
        in_pair = ([saved[s][9] for s in range(2)], [held[1 - s][0] for s in range(2)])
        back_pair = ([saved[s][10] for s in range(2)], [held[1 - s][1] for s in range(2)])
        in_got = swap_section(expert_grads(*in_pair, 1 - own_layer, [], BF16))
        back_got = swap_section(expert_grads(*back_pair, 1 - own_layer, [], BF16))
        in_grad = expert_grads(*in_pair, own_layer, [in_got], F32)
        back_grad = expert_grads(*back_pair, own_layer, [back_got], F32)
        out_sum = whole_grad(held[1][2], held[0][2])
        small_sum = whole_grad(held[1][3], held[0][3])
        tall = jnp.concatenate(
            [out_sum, jnp.broadcast_to(small_sum[None], (devices,) + small_sum.shape)], axis=1
        ).astype(BF16)
        return (sum_blocks(exchange_tensor([tall[d] for d in range(devices)])), (in_grad, back_grad))

    def attention_part(qkv_grad, rel_grad, tall):
        held = held_attention
        held.append((qkv_grad, rel_grad))
        if len(held) < 2:
            return ()
        wide = jnp.concatenate([whole_grad(qkv_grad, held[0][0]), tall.T], axis=1)
        rel_sum = whole_grad(rel_grad, held[0][1])
        rel_wide = jnp.pad(rel_sum, ((0, 0), (0, wide.shape[1] - rel_sum.shape[1])))
        packed = jnp.concatenate(
            [wide.reshape(groups, -1, wide.shape[1]), rel_wide.reshape(groups, -1, wide.shape[1])],
            axis=1,
        ).astype(BF16)
        shares = jnp.sum(swap_experts(packed).astype(F32), axis=0)
        return (
            shares[:mine, 4 * cols][None],
            shares[:mine, :cols][None],
            shares[:mine, cols : 2 * cols][None],
            shares[:mine, 2 * cols : 3 * cols][None],
            shares[:mine, 3 * cols : 4 * cols].T[None],
            shares[mine:, : rel_bias.shape[2]][None],
            shares[:mine, 4 * cols + 1 :][None],
        )

    grads = [None, None]
    row_grads = [None, None]
    rows = pick(cotangent, core)
    for s in (1, 0):
        rows, grads[s] = layer_backward(
            saved[s],
            rows,
            weights[s],
            rels[s],
            plans[s],
            ahead if s == 1 else None,
            gates,
            (expert_part, attention_part),
        )
        row_grads[s] = rows

    def whole_rows(pair):
        own = jnp.where(first, pair[0], pair[1])
        got = swap_section(jnp.where(first, pair[1], pair[0]))
        result = jnp.zeros((2,) + own.shape, own.dtype)
        result = lax.dynamic_update_index_in_dim(result, own, core, 0)
        return lax.dynamic_update_index_in_dim(result, got, 1 - core, 0)[None]

    attn_grad = whole_grad(grads[0][0], grads[1][0])
    attn_grad = sum_blocks(exchange_tensor([attn_grad] * devices))
    attn_grad = jnp.sum(swap_experts(attn_grad.reshape(groups, -1)), axis=0)
    in_grad, back_grad = grads[0][1]
    return (
        whole_rows(acts),
        whole_rows(row_grads),
        attn_grad[None],
        *grads[0][2],
        in_grad[None],
        back_grad[None],
    )


def solution(mesh):
    placed = (
        P(None, "expert", None),
        P(None, "expert", None),
        P("section", None),
        P("section", None),
        P("section", None, "tensor"),
        P("section", None, "tensor"),
        P("section", None, "tensor"),
        P("section", "tensor", None),
        P("section", None, "tensor"),
        P("section", None, None),
        P("section", "expert", None, "tensor"),
        P("section", "expert", "tensor", None),
        P("section", None, "expert", None),
        P("section", None, "expert"),
    )
    return jax.shard_map(
        body,
        mesh=mesh,
        in_specs=placed,
        out_specs=(
            P("section", None, "expert", None),
            P("section", None, "expert", None),
            P("section", "expert"),
            P("section", "expert"),
            P("section", "expert", "tensor"),
            P("section", "expert", "tensor"),
            P("section", "expert", "tensor"),
            P("section", "tensor", "expert"),
            P("section", "expert", "tensor"),
            P("section", "expert", None),
            P("section", "expert", None, "tensor"),
            P("section", "expert", "tensor", None),
        ),
        check_vma=False,
    )
```

```python
import functools
import jax
import jax.numpy as jnp
import numpy as np
from jax import lax
from jax.experimental import pallas as pl
from jax.experimental.pallas import tpu as pltpu
from jax.sharding import PartitionSpec as P

DH = 64
LENGTH = 512
TILE = 128
EPSILON = 1e-06
BF16 = jnp.bfloat16
F32 = jnp.float32


def bucket_starts():
    starts = list(range(1, 9))
    for ladder in range(1, 8):
        distance = 8
        while distance**8 < 2 ** (24 + 4 * ladder):
            distance = distance + 1
        starts.append(distance)
    return starts


STARTS = bucket_starts()
HALF = len(STARTS) + 1


def root_mean(values):
    return lax.rsqrt(jnp.mean(values * values, axis=-1, keepdims=True) + EPSILON)


def dot(left, right):
    return jnp.dot(left, right, preferred_element_type=F32)


def dot_left(left, right):
    return lax.dot_general(left, right, (((0,), (0,)), ((), ())), preferred_element_type=F32)


def dot_right(left, right):
    return lax.dot_general(left, right, (((1,), (1,)), ((), ())), preferred_element_type=F32)


def offset_block(delta):
    rows = lax.broadcasted_iota(jnp.int32, (TILE, TILE), 0)
    cols = lax.broadcasted_iota(jnp.int32, (TILE, TILE), 1)
    return rows - cols + delta * TILE


def fill_bias(rel_ref, bias_ref, heads):
    tiles = LENGTH // TILE
    for delta in (-1, 0, 1):
        offset = offset_block(delta)
        blocks = [jnp.full((TILE, TILE), rel_ref[0, h], F32) for h in range(heads)]
        for step, start in enumerate(STARTS):
            if delta <= 0:
                mask = offset <= -start
                blocks = [
                    jnp.where(mask, rel_ref[step + 1, h], block) for h, block in enumerate(blocks)
                ]
            if delta >= 0:
                mask = offset >= start
                blocks = [
                    jnp.where(mask, rel_ref[HALF + step + 1, h], block)
                    for h, block in enumerate(blocks)
                ]
        for h in range(heads):
            for i in range(tiles):
                j = i - delta
                if 0 <= j < tiles:
                    bias_ref[h, i * TILE : (i + 1) * TILE, j * TILE : (j + 1) * TILE] = blocks[h]
    for h in range(heads):
        above = jnp.full((TILE, TILE), rel_ref[2 * HALF - 1, h], F32)
        below = jnp.full((TILE, TILE), rel_ref[HALF - 1, h], F32)
        for i in range(tiles):
            for j in range(tiles):
                if abs(i - j) > 1:
                    bias_ref[h, i * TILE : (i + 1) * TILE, j * TILE : (j + 1) * TILE] = (
                        above if i > j else below
                    )


def attend_kernel(rel_ref, qkv_ref, mixed_ref, lse_ref, bias_ref, *, heads):
    @pl.when(pl.program_id(0) == 0)
    def _():
        fill_bias(rel_ref, bias_ref, heads)

    cols = heads * DH
    outs = []
    for h in range(heads):
        query = qkv_ref[:, h * DH : (h + 1) * DH]
        keys = qkv_ref[:, cols + h * DH : cols + (h + 1) * DH]
        values = qkv_ref[:, 2 * cols + h * DH : 2 * cols + (h + 1) * DH]
        scores = dot_right(keys, query) * 0.125 + bias_ref[h]
        highest = jnp.max(scores, axis=0, keepdims=True)
        raised = jnp.exp(scores - highest)
        total = jnp.sum(raised, axis=0, keepdims=True)
        probs = (raised * (1.0 / total)).astype(BF16)
        outs.append(dot_left(probs, values).astype(BF16))
        lse_ref[0, h : h + 1, :] = highest + jnp.log(total)
    mixed_ref[...] = jnp.concatenate(outs, axis=1)


def attend(qkv, rel):
    rows = qkv.shape[0]
    heads = rel.shape[1]
    cols = heads * DH
    sequences = rows // LENGTH
    return pl.pallas_call(
        functools.partial(attend_kernel, heads=heads),
        grid=(sequences,),
        in_specs=[
            pl.BlockSpec(memory_space=pltpu.SMEM),
            pl.BlockSpec((LENGTH, 3 * cols), lambda s: (s, 0)),
        ],
        out_specs=[
            pl.BlockSpec((LENGTH, cols), lambda s: (s, 0)),
            pl.BlockSpec((1, heads, LENGTH), lambda s: (s, 0, 0)),
        ],
        out_shape=[
            jax.ShapeDtypeStruct((rows, cols), BF16),
            jax.ShapeDtypeStruct((sequences, heads, LENGTH), F32),
        ],
        scratch_shapes=[pltpu.VMEM((heads, LENGTH, LENGTH), F32)],
        compiler_params=pltpu.CompilerParams(
            dimension_semantics=("arbitrary",), vmem_limit_bytes=40 << 20
        ),
    )(rel, qkv)


def attend_back_kernel(
    rel_ref, qkv_ref, lse_ref, grad_ref, dqkv_ref, drel_ref, bias_ref, near_ref, *, heads
):
    tiles = LENGTH // TILE

    @pl.when(pl.program_id(0) == 0)
    def _():
        fill_bias(rel_ref, bias_ref, heads)
        near_ref[...] = jnp.zeros_like(near_ref)

    cols = heads * DH
    dqs, dks, dvs = [], [], []
    for h in range(heads):
        query = qkv_ref[:, h * DH : (h + 1) * DH]
        keys = qkv_ref[:, cols + h * DH : cols + (h + 1) * DH]
        values = qkv_ref[:, 2 * cols + h * DH : 2 * cols + (h + 1) * DH]
        grad = grad_ref[:, h * DH : (h + 1) * DH]
        scores = dot_right(keys, query) * 0.125 + bias_ref[h]
        probs = jnp.exp(scores - lse_ref[0, h : h + 1, :])
        dvs.append(dot(probs.astype(BF16), grad).astype(BF16))
        dprobs = dot_right(values, grad)
        weighted = jnp.sum(probs * dprobs, axis=0, keepdims=True)
        dscores = (probs * (dprobs - weighted)).astype(BF16)
        dks.append((dot(dscores, query) * 0.125).astype(BF16))
        dqs.append((dot_left(dscores, keys) * 0.125).astype(BF16))
        wide = dscores.astype(F32)
        sums = [None] * 5
        for i in range(tiles):
            for j in range(tiles):
                place = max(-2, min(2, i - j)) + 2
                block = wide[i * TILE : (i + 1) * TILE, j * TILE : (j + 1) * TILE]
                sums[place] = block if sums[place] is None else sums[place] + block
        for place in range(5):
            near_ref[h, place] = near_ref[h, place] + sums[place]
    dqkv_ref[...] = jnp.concatenate(dqs + dks + dvs, axis=1)

    @pl.when(pl.program_id(0) == pl.num_programs(0) - 1)
    def _():
        edges = STARTS + [1 << 20]
        for h in range(heads):
            rows = [jnp.zeros((1, TILE), F32) for _ in range(2 * HALF)]
            for delta in (-1, 0, 1):
                offset = offset_block(delta)
                block = near_ref[h, delta + 2]
                if delta == 0:
                    rows[0] = jnp.sum(
                        jnp.where(offset == 0, block, 0.0), axis=0, keepdims=True
                    )
                for step in range(HALF - 1):
                    if delta <= 0:
                        mask = (offset <= -edges[step]) & (offset > -edges[step + 1])
                        rows[step + 1] = rows[step + 1] + jnp.sum(
                            jnp.where(mask, block, 0.0), axis=0, keepdims=True
                        )
                    if delta >= 0:
                        mask = (offset >= edges[step]) & (offset < edges[step + 1])
                        rows[HALF + step + 1] = rows[HALF + step + 1] + jnp.sum(
                            jnp.where(mask, block, 0.0), axis=0, keepdims=True
                        )
            rows[HALF - 1] = rows[HALF - 1] + jnp.sum(near_ref[h, 0], axis=0, keepdims=True)
            rows[2 * HALF - 1] = rows[2 * HALF - 1] + jnp.sum(
                near_ref[h, 4], axis=0, keepdims=True
            )
            drel_ref[h] = jnp.concatenate(rows, axis=0)


def attend_back(qkv, rel, lse, grad):
    rows = qkv.shape[0]
    heads = rel.shape[1]
    cols = heads * DH
    sequences = rows // LENGTH
    return pl.pallas_call(
        functools.partial(attend_back_kernel, heads=heads),
        grid=(sequences,),
        in_specs=[
            pl.BlockSpec(memory_space=pltpu.SMEM),
            pl.BlockSpec((LENGTH, 3 * cols), lambda s: (s, 0)),
            pl.BlockSpec((1, heads, LENGTH), lambda s: (s, 0, 0)),
            pl.BlockSpec((LENGTH, cols), lambda s: (s, 0)),
        ],
        out_specs=[
            pl.BlockSpec((LENGTH, 3 * cols), lambda s: (s, 0)),
            pl.BlockSpec((heads, 2 * HALF, TILE), lambda s: (0, 0, 0)),
        ],
        out_shape=[
            jax.ShapeDtypeStruct((rows, 3 * cols), BF16),
            jax.ShapeDtypeStruct((heads, 2 * HALF, TILE), F32),
        ],
        scratch_shapes=[
            pltpu.VMEM((heads, LENGTH, LENGTH), F32),
            pltpu.VMEM((heads, 5, TILE, TILE), F32),
        ],
        compiler_params=pltpu.CompilerParams(
            dimension_semantics=("arbitrary",), vmem_limit_bytes=40 << 20
        ),
    )(rel, qkv, lse, grad)


def swap_tensor(block, distance):
    devices = lax.axis_size("tensor")
    return lax.ppermute(block, "tensor", [(i, i ^ distance) for i in range(devices)])


def gather_tensor(block):
    return [block] + [swap_tensor(block, d) for d in range(1, lax.axis_size("tensor"))]


def exchange_tensor(blocks):
    return [blocks[0]] + [swap_tensor(blocks[d], d) for d in range(1, len(blocks))]


def swap_section(block):
    return lax.ppermute(block, "section", [(0, 1), (1, 0)])


def swap_experts(block):
    return lax.all_to_all(block, "expert", split_axis=0, concat_axis=0, tiled=True)


def sum_blocks(blocks):
    total = blocks[0].astype(F32)
    for block in blocks[1:]:
        total = total + block.astype(F32)
    return total


def chunks_of(local):
    return 1


def make_plan(route_rows, keep_rows, experts, capacity):
    tokens = route_rows.shape[0]
    devices = lax.axis_size("tensor")
    rank = lax.axis_index("tensor")
    owned = tokens // devices
    share = capacity // devices
    ids = jnp.arange(experts, dtype=jnp.int32)
    chosen = route_rows[:, None] == ids[None, :]
    order = jnp.arange(tokens, dtype=jnp.int32)
    lower = (order[:, None] > order[None, :]).astype(BF16)
    before = dot(lower, chosen.astype(BF16))
    chosen_f = chosen.astype(F32)
    counts = jnp.sum(chosen_f, axis=0)
    starts = jnp.sum(jnp.where(ids[None, :] < ids[:, None], counts[None, :], 0.0), axis=1)
    position = jnp.sum(chosen_f * (before + starts[None, :]), axis=1).astype(jnp.int32)
    distances = jnp.arange(devices, dtype=jnp.int32)
    rows = jnp.arange(owned, dtype=jnp.int32)
    wanted = (rows[None, :] * devices + (rank ^ distances)[:, None]).reshape(-1)
    deal = (wanted[:, None] == position[None, :]).astype(BF16)
    mine = wanted[:owned, None] == position[None, :]
    route_own = jnp.sum(jnp.where(mine, route_rows[None, :], 0), axis=1, dtype=jnp.int32)
    keep_own = jnp.sum(jnp.where(mine, keep_rows[None, :], 0), axis=1, dtype=jnp.int32)
    chosen_own = route_own[:, None] == ids[None, :]
    first = (starts.astype(jnp.int32) - rank + devices - 1) // devices
    slot = rows - jnp.sum(jnp.where(chosen_own, first[None, :], 0), axis=1, dtype=jnp.int32)
    slot = jnp.where(keep_own > 0, route_own * share + slot, -1)
    groups = lax.axis_size("expert")
    local = experts // groups
    chunks = chunks_of(local)
    ahead = (lax.axis_index("expert") + jnp.arange(groups, dtype=jnp.int32)) % groups
    inner = np.arange(local * share, dtype=np.int32).reshape(chunks, -1)
    places = []
    for chunk in inner:
        wanted_slot = (ahead[:, None] * (local * share) + chunk[None, :]).reshape(-1)
        places.append((wanted_slot[:, None] == slot[None, :]).astype(BF16))
    return (deal, deal[:owned], places, chosen_own.astype(F32), keep_own.astype(F32))


def shift_experts(block, distance):
    groups = lax.axis_size("expert")
    if distance % groups == 0:
        return block
    return lax.ppermute(block, "expert", [(i, (i + distance) % groups) for i in range(groups)])


def to_groups(rows, local):
    groups = lax.axis_size("expert")
    rows = rows.reshape(groups, local, -1, rows.shape[1])
    return jnp.concatenate([shift_experts(rows[d], d) for d in range(groups)], axis=1)


def send_tokens(rows, places, local):
    per_chunk = local // len(places)
    return [to_groups(dot(place, rows).astype(BF16), per_chunk) for place in places]


def from_experts(parts, place):
    groups = lax.axis_size("expert")
    local, own, width = parts[0].shape
    blocks = exchange_tensor(parts)
    summed = sum_blocks(blocks).astype(BF16)
    share = own // groups
    back = [
        shift_experts(summed[:, d * share : (d + 1) * share].reshape(-1, width), -d)
        for d in range(groups)
    ]
    return dot_left(place, jnp.concatenate(back, axis=0))


def ffn_kernel(*refs, devices):
    blocks, first_ref, second_ref = refs[:devices], refs[devices], refs[devices + 1]
    rows_ref, hidden_ref, slope_ref = refs[devices + 2 : devices + 5]
    parts = refs[devices + 5 :]
    size = blocks[0].shape[1]
    for d in range(devices):
        rows_ref[0, d * size : (d + 1) * size, :] = blocks[d][0]
    inner = dot(rows_ref[0], first_ref[0, 0])
    cumulative = 0.5 * (1.0 + lax.erf(inner * np.float32(np.sqrt(0.5))))
    density = jnp.exp(-0.5 * inner * inner) * np.float32(1.0 / np.sqrt(2.0 * np.pi))
    hidden = (inner * cumulative).astype(BF16)
    hidden_ref[0] = hidden
    slope_ref[0] = (cumulative + inner * density).astype(BF16)
    out = dot(hidden, second_ref[0, 0]).astype(BF16)
    for d in range(devices):
        parts[d][0] = out[d * size : (d + 1) * size]


def ffn_back_kernel(*refs, devices, gated):
    blocks, refs = refs[:devices], refs[devices:]
    if gated:
        factor_ref, refs = refs[0], refs[1:]
    first_ref, second_ref, slope_ref, grad_ref, inner_ref = refs[:5]
    parts = refs[5:]
    size = blocks[0].shape[1]
    for d in range(devices):
        block = blocks[d][0]
        if gated:
            factor = factor_ref[0, d * size : (d + 1) * size, :]
            block = (factor * block.astype(F32)).astype(BF16)
        grad_ref[0, d * size : (d + 1) * size, :] = block
    hidden_grad = dot_right(grad_ref[0], second_ref[0, 0])
    inner_grad = (hidden_grad * slope_ref[0].astype(F32)).astype(BF16)
    inner_ref[0] = inner_grad
    out = dot_right(inner_grad, first_ref[0, 0]).astype(BF16)
    for d in range(devices):
        parts[d][0] = out[d * size : (d + 1) * size]


def ffn_call(kernel, blocks, weights, others, widths):
    first, second, layer, start = weights
    devices = len(blocks)
    count, size, width = blocks[0].shape
    slots = devices * size
    inner = first.shape[3]

    def rows(height, cols):
        return pl.BlockSpec((1, height, cols), lambda e: (e, 0, 0))

    def weight(array):
        return pl.BlockSpec((1, 1) + array.shape[2:], lambda e: (layer, start + e, 0, 0))

    before = [other for other in others if other.shape[2] == 1]
    after = [other for other in others if other.shape[2] != 1]
    return pl.pallas_call(
        kernel,
        grid=(count,),
        in_specs=[rows(size, width)] * devices
        + [rows(slots, 1) for _ in before]
        + [weight(first), weight(second)]
        + [rows(slots, other.shape[2]) for other in after],
        out_specs=[rows(slots, cols) for cols in widths] + [rows(size, width)] * devices,
        out_shape=[jax.ShapeDtypeStruct((count, slots, cols), BF16) for cols in widths]
        + [jax.ShapeDtypeStruct((count, size, width), BF16)] * devices,
        compiler_params=pltpu.CompilerParams(
            dimension_semantics=("arbitrary",), vmem_limit_bytes=40 << 20
        ),
        cost_estimate=pl.CostEstimate(
            flops=4 * count * slots * width * inner,
            transcendentals=2 * count * slots * inner,
            bytes_accessed=4 * count * (width * inner + 2 * slots * width),
        ),
    )(*blocks, *before, first, second, *after)


def grads_kernel(pick_ref, *refs, chunks, per_chunk):
    lefts, rights = refs[: 2 * chunks], refs[2 * chunks : 4 * chunks]
    extra, out_ref = refs[4 * chunks : -1], refs[-1]
    expert = pl.program_id(0)
    for layer in range(2):
        for c in range(chunks):

            @pl.when((pick_ref[0] == layer) & (expert // per_chunk == c))
            def _():
                value = dot_left(lefts[layer * chunks + c][0], rights[layer * chunks + c][0])
                for ref in extra:
                    value = value + ref[0].astype(F32)
                out_ref[0] = value.astype(out_ref.dtype)


def expert_grads(lefts, rights, layer, extra, kind):
    chunks = len(lefts[0])
    per_chunk, slots, rows = lefts[0][0].shape
    cols = rights[0][0].shape[2]
    local = chunks * per_chunk

    def spec(owner, c, width):
        def place(e, pick):
            own = jnp.clip(e - c * per_chunk, 0, per_chunk - 1)
            return (jnp.where(pick[0] == owner, own, 0), 0, 0)

        return pl.BlockSpec((1, slots, width), place)

    whole = pl.BlockSpec((1, rows, cols), lambda e, pick: (e, 0, 0))
    names = [(owner, c) for owner in range(2) for c in range(chunks)]
    return pl.pallas_call(
        functools.partial(grads_kernel, chunks=chunks, per_chunk=per_chunk),
        grid_spec=pltpu.PrefetchScalarGridSpec(
            num_scalar_prefetch=1,
            grid=(local,),
            in_specs=[spec(owner, c, rows) for owner, c in names]
            + [spec(owner, c, cols) for owner, c in names]
            + [whole] * len(extra),
            out_specs=whole,
        ),
        out_shape=jax.ShapeDtypeStruct((local, rows, cols), kind),
        compiler_params=pltpu.CompilerParams(
            dimension_semantics=("arbitrary",), vmem_limit_bytes=40 << 20
        ),
        cost_estimate=pl.CostEstimate(
            flops=2 * local * slots * rows * cols,
            transcendentals=0,
            bytes_accessed=local * (6 * rows * cols + 2 * slots * (rows + cols)),
        ),
    )(layer, *lefts[0], *lefts[1], *rights[0], *rights[1], *extra)


def layer_forward(rows_in, weights, rel, plan, ahead, with_gates):
    attn_gain, ffn_gain, w_qkv, w_out, w_router, w_in, w_back, layer = weights
    deal, deal_own, places, chosen, kept = plan
    devices = lax.axis_size("tensor")
    local, width, inner_width = w_in.shape[1:]
    layer_in = rows_in.astype(F32)
    scale_one = root_mean(layer_in)
    normed = (layer_in * scale_one * attn_gain).astype(BF16)
    qkv = dot(normed, w_qkv).astype(BF16)
    mixed, lse = attend(qkv, rel)
    if with_gates:
        mixed, ahead = lax.optimization_barrier((mixed, ahead))
    cols = mixed.shape[1]
    dealt = dot(deal, mixed).astype(BF16).reshape(devices, -1, cols)
    heads = exchange_tensor([dealt[d] for d in range(devices)])
    own_in = dot(deal_own, rows_in)
    branch = sum(dot(heads[d], w_out[d]) for d in range(devices))
    middle = own_in + branch
    scale_two = root_mean(middle)
    normed_two = (middle * scale_two * ffn_gain).astype(BF16)
    probs = jax.nn.softmax(dot(normed_two, w_router), axis=-1)
    gate = jnp.sum(probs * chosen, axis=-1)
    gates = send_gates(kept * gate, places, local) if with_gates else None
    sent = [gather_tensor(got) for got in send_tokens(normed_two, places, local)]
    if not with_gates:
        sent[-1], ahead = lax.optimization_barrier((sent[-1], ahead))
    incoming, hidden, slope, per_token = [], [], [], 0.0
    for n, place in enumerate(places):
        chosen_weights = (w_in, w_back, layer, n * local // len(places))
        rows, low, steep, *parts = ffn_call(
            functools.partial(ffn_kernel, devices=devices),
            sent[n],
            chosen_weights,
            [],
            (width, inner_width, inner_width),
        )
        incoming.append(rows)
        hidden.append(low)
        slope.append(steep)
        if with_gates:
            parts, gates = lax.optimization_barrier((parts, gates))
        per_token = per_token + from_experts(parts, place)
    output = (middle + (kept * gate)[:, None] * per_token).astype(BF16)
    every = jnp.concatenate(gather_tensor(output), axis=0)
    rows_out = dot_left(deal, every).astype(BF16)
    saved = (own_in, normed, qkv, lse, heads, middle, normed_two, probs, gate)
    return (rows_out, saved + (incoming, hidden, slope, per_token), ahead, gates)


def norm_back(grad, values, gain):
    scale = root_mean(values)
    scaled = grad * gain
    values_grad = scale * scaled - values * (scale * scale * scale) * jnp.mean(
        scaled * values, axis=-1, keepdims=True
    )
    return (values_grad, jnp.sum(grad * values * scale, axis=0))


def send_gates(gates, places, local):
    groups = lax.axis_size("expert")
    factors = [
        jnp.sum(place.astype(F32) * gates[None, :], axis=1).reshape(groups, local // len(places), -1)
        for place in places
    ]
    factors = jnp.concatenate(factors, axis=1)
    got = jnp.concatenate([shift_experts(factors[d], d) for d in range(groups)], axis=1)
    got = jnp.concatenate(gather_tensor(got), axis=1)
    return jnp.split(got[:, :, None], len(places))


def layer_backward(saved, rows_grad, weights, rel, plan, early, gates, finish):
    attn_gain, ffn_gain, w_qkv, w_out, w_router, w_in, w_back, layer = weights
    deal, deal_own, places, chosen, kept = plan
    own_in, normed, qkv, lse, heads, middle, normed_two, probs, gate = saved[:9]
    incoming, hidden, slope, per_token = saved[9:]
    devices = lax.axis_size("tensor")
    local, width, inner_width = w_in.shape[1:]
    grad_out = dot(deal_own, rows_grad)
    gated = ((kept * gate)[:, None] * grad_out).astype(BF16)
    gate_grad = kept * jnp.sum(grad_out * per_token, axis=-1)
    if early is None:
        early = [gather_tensor(got) for got in send_tokens(gated, places, local)]
        gates = None
    input_rows, inner_grads, expert_grad = 0.0, [], []
    for n, place in enumerate(places):
        rows, low, *parts = ffn_call(
            functools.partial(ffn_back_kernel, devices=devices, gated=gates is not None),
            early[n],
            (w_in, w_back, layer, n * local // len(places)),
            ([] if gates is None else [gates[n]]) + [slope[n]],
            (width, inner_width),
        )
        expert_grad.append(rows)
        inner_grads.append(low)
        input_rows = input_rows + from_experts(parts, place)
    logit_grad = (probs * (chosen - gate[:, None]) * gate_grad[:, None]).astype(BF16)
    router_grad = dot_left(normed_two, logit_grad)
    normed_two_grad = input_rows + dot_right(logit_grad, w_router)
    middle_part, ffn_grad = norm_back(normed_two_grad, middle, ffn_gain)
    middle_grad = grad_out + middle_part
    branch_grad = middle_grad.astype(BF16)
    head_grads = exchange_tensor(
        [dot_right(branch_grad, w_out[d]).astype(BF16) for d in range(devices)]
    )
    mixed_grad = dot_left(deal, jnp.concatenate(head_grads, axis=0)).astype(BF16)
    out_grad = jnp.stack([dot_left(heads[d], branch_grad) for d in range(devices)])
    small = jnp.concatenate([ffn_grad[None], router_grad.T], axis=0)
    beside, fill = finish[0](inner_grads, expert_grad, out_grad, small)
    dqkv, drel = attend_back(qkv, rel, lse, mixed_grad)
    dqkv, beside = lax.optimization_barrier((dqkv, beside))
    qkv_grad = dot_left(normed, dqkv)
    rel_grad = jnp.sum(drel, axis=-1).T
    normed_parts = dot_right(dot(deal, dqkv).astype(BF16), w_qkv).astype(BF16)
    normed_parts = normed_parts.reshape(devices, -1, normed_parts.shape[1])
    blocks = exchange_tensor([normed_parts[d] for d in range(devices)])
    blocks, fill = lax.optimization_barrier((blocks, fill))
    normed_grad = sum_blocks(blocks)
    layer_part, attn_grad = norm_back(normed_grad, own_in, attn_gain)
    layer_grad = (middle_grad + layer_part).astype(BF16)
    last, loose = finish[1](qkv_grad, rel_grad, attn_grad, beside)
    blocks, last = lax.optimization_barrier((gather_tensor(layer_grad), last))
    rows_out = dot_left(deal, jnp.concatenate(blocks, axis=0)).astype(BF16)
    return (rows_out, (fill, loose, last))


def body(
    x_in,
    cotangent,
    attn_gain,
    ffn_gain,
    w_query,
    w_key,
    w_value,
    w_out,
    rel_bias,
    w_router,
    w_in,
    w_back,
    routes,
    keep_mask,
):
    core = lax.axis_index("section")
    first = core == 0
    groups = lax.axis_size("expert")
    devices = lax.axis_size("tensor")
    experts = w_router.shape[2]
    tokens = x_in.shape[1]
    width = x_in.shape[2]
    capacity = 3 * tokens // (2 * experts)

    def both(own):
        other = swap_section(own)
        return (jnp.where(first, own, other), jnp.where(first, other, own))

    def pick(stack, index):
        return lax.dynamic_index_in_dim(stack, index, 0, keepdims=False)

    qkv_pair = both(jnp.concatenate([w_query[0], w_key[0], w_value[0]], axis=1))
    rel_pair = both(rel_bias[0])
    attn_pair = both(attn_gain)
    ffn_pair = both(ffn_gain)
    router_pair = both(w_router[0])
    out_pair = both(jnp.stack(gather_tensor(w_out[0])))
    in_all = lax.all_gather(w_in[0], "section", axis=0)
    back_all = lax.all_gather(w_back[0], "section", axis=0)
    own_ints = jnp.stack([pick(routes[0], core)[:, 0], pick(keep_mask[0], core)])
    sent_ints = jnp.stack([pick(routes[0], 1 - core)[:, 0], pick(keep_mask[0], 1 - core)])
    got_ints = swap_section(sent_ints)
    ints_pair = (jnp.where(first, own_ints, got_ints), jnp.where(first, got_ints, own_ints))

    weights, rels, plans = [], [], []
    for s in range(2):
        weights.append(
            (
                attn_pair[s][0].astype(F32),
                ffn_pair[s][0].astype(F32),
                qkv_pair[s],
                out_pair[s],
                router_pair[s],
                in_all,
                back_all,
                s,
            )
        )
        rels.append(rel_pair[s].astype(F32))
        plans.append(make_plan(ints_pair[s][0], ints_pair[s][1], experts, capacity))

    ahead = send_tokens(
        dot(plans[1][1], pick(cotangent, core)).astype(BF16), plans[1][2], w_in.shape[1]
    )
    rows = pick(x_in, core)
    acts, saved = [], []
    for s in range(2):
        rows, kept, ahead, gates = layer_forward(rows, weights[s], rels[s], plans[s], ahead, s == 1)
        if s == 0:
            ahead = [gather_tensor(got) for got in ahead]
        acts.append(rows)
        saved.append(kept)
    def whole_grad(low, high):
        got = swap_section(jnp.where(first, high, low).astype(BF16))
        return jnp.where(first, low, high) + got.astype(F32)

    own_layer = core.reshape(1)
    mine = width // groups
    cols = w_query.shape[2]
    def whole_rows(pair):
        own = jnp.where(first, pair[0], pair[1])
        got = swap_section(jnp.where(first, pair[1], pair[0]))
        result = jnp.zeros((2,) + own.shape, own.dtype)
        result = lax.dynamic_update_index_in_dim(result, own, core, 0)
        return lax.dynamic_update_index_in_dim(result, got, 1 - core, 0)[None]

    held_experts, held_attention = [], []

    def expert_part(inner_grads, expert_grad, out_grad, small):
        held = held_experts
        held.append((inner_grads, expert_grad, out_grad, small))
        if len(held) < 2:
            return ((out_grad, small), ())
        in_pair = ([saved[s][9] for s in range(2)], [held[1 - s][0] for s in range(2)])
        back_pair = ([saved[s][10] for s in range(2)], [held[1 - s][1] for s in range(2)])
        in_got = swap_section(expert_grads(*in_pair, 1 - own_layer, [], BF16))
        back_got = swap_section(expert_grads(*back_pair, 1 - own_layer, [], BF16))
        in_grad = expert_grads(*in_pair, own_layer, [in_got], F32)
        back_grad = expert_grads(*back_pair, own_layer, [back_got], F32)
        out_sum = whole_grad(held[1][2], held[0][2])
        small_sum = whole_grad(held[1][3], held[0][3])
        tall = jnp.concatenate(
            [out_sum, jnp.broadcast_to(small_sum[None], (devices,) + small_sum.shape)], axis=1
        ).astype(BF16)
        return (sum_blocks(exchange_tensor([tall[d] for d in range(devices)])), (in_grad, back_grad))

    def attention_part(qkv_grad, rel_grad, attn_grad, tall):
        held = held_attention
        held.append((qkv_grad, rel_grad, attn_grad))
        if len(held) < 2:
            return ((), ())
        wide = jnp.concatenate([whole_grad(qkv_grad, held[0][0]), tall.T], axis=1)
        rel_sum = whole_grad(rel_grad, held[0][1])
        rel_wide = jnp.pad(rel_sum, ((0, 0), (0, wide.shape[1] - rel_sum.shape[1])))
        packed = jnp.concatenate(
            [wide.reshape(groups, -1, wide.shape[1]), rel_wide.reshape(groups, -1, wide.shape[1])],
            axis=1,
        ).astype(BF16)
        shares = jnp.sum(swap_experts(packed).astype(F32), axis=0)
        attn_sum = sum_blocks(exchange_tensor([whole_grad(attn_grad, held[0][2])] * devices))
        attn_sum = jnp.sum(swap_experts(attn_sum.reshape(groups, -1)), axis=0)
        tied = (
            shares[:mine, 4 * cols][None],
            shares[:mine, :cols][None],
            shares[:mine, cols : 2 * cols][None],
            shares[:mine, 2 * cols : 3 * cols][None],
            shares[:mine, 3 * cols : 4 * cols].T[None],
            shares[mine:, : rel_bias.shape[2]][None],
            shares[:mine, 4 * cols + 1 :][None],
        )
        return (tied, (attn_sum[None],))

    grads = [None, None]
    row_grads = [None, None]
    rows = pick(cotangent, core)
    for s in (1, 0):
        rows, grads[s] = layer_backward(
            saved[s],
            rows,
            weights[s],
            rels[s],
            plans[s],
            ahead if s == 1 else None,
            gates,
            (expert_part, attention_part),
        )
        row_grads[s] = rows

    in_grad, back_grad = grads[0][0]
    return (
        whole_rows(acts),
        whole_rows(row_grads),
        *grads[0][1],
        *grads[0][2],
        in_grad[None],
        back_grad[None],
    )


def solution(mesh):
    placed = (
        P(None, "expert", None),
        P(None, "expert", None),
        P("section", None),
        P("section", None),
        P("section", None, "tensor"),
        P("section", None, "tensor"),
        P("section", None, "tensor"),
        P("section", "tensor", None),
        P("section", None, "tensor"),
        P("section", None, None),
        P("section", "expert", None, "tensor"),
        P("section", "expert", "tensor", None),
        P("section", None, "expert", None),
        P("section", None, "expert"),
    )
    return jax.shard_map(
        body,
        mesh=mesh,
        in_specs=placed,
        out_specs=(
            P("section", None, "expert", None),
            P("section", None, "expert", None),
            P("section", "expert"),
            P("section", "expert"),
            P("section", "expert", "tensor"),
            P("section", "expert", "tensor"),
            P("section", "expert", "tensor"),
            P("section", "tensor", "expert"),
            P("section", "expert", "tensor"),
            P("section", "expert", None),
            P("section", "expert", None, "tensor"),
            P("section", "expert", "tensor", None),
        ),
        check_vma=False,
    )
```
